32 devices in a mesh: seq: 4 (over z), tp: 4 (over x, core), dp: 2 (over y).
Axes of the slice: x: 2, y: 2, z: 4, core: 2. Of those that a mesh axis runs over, the one named last changes fastest.
Arguments:
- queries: bfloat16 [2, 512, 4096], P('dp', 'seq', 'tp'), may hold values from -0.5 to 0.5
- keys: bfloat16 [2, 512, 4096], P('dp', 'seq', 'tp'), may hold values from -0.25 to 0.25
- values: bfloat16 [2, 512, 4096], P('dp', 'seq', 'tp'), may hold values from -19 to 19
- out_gain: float32 [4096], P('tp'), may hold values from 0.1 to 1.9
- grad_out: bfloat16 [2, 512, 4096], P('dp', 'seq', 'tp'), may hold values from -12 to 12
Outputs:
- normed: bfloat16 [2, 512, 4096], P('dp', 'seq', 'tp')
- query_gradient: bfloat16 [2, 512, 4096], P('dp', 'seq', 'tp')
- grad_keys: bfloat16 [2, 512, 4096], P('dp', 'seq', 'tp')
- value_gradient: bfloat16 [2, 512, 4096], P('dp', 'seq', 'tp')
- gain_grad: float32 [4096], P('tp')
The draws below stay inside these ranges and needn't reach their ends.
All inputs are finite; a program needn't handle non-finite values.
Results may differ from the reference program's by a relative error of at most 0.005.
Values sent between devices are 32-bit elements; how exact they have to be, the bound alone decides.
A program may use at most 64 MiB of HBM per device.

```python
import jax
import jax.numpy as jnp
from jax import lax

HEADS = 32
HD = 128
HID = 4096
BLOCK = 128
TOKENS = 512
SEQS = 2


def rough_base(base_key, shape, bound):
    return jnp.clip(jax.random.normal(base_key, shape, jnp.float32), -bound, bound)


def draw_values(key, part):
    own_key = jax.random.fold_in(key, 17)
    base_key, jitter_key = jax.random.split(own_key, 2)
    base = rough_base(base_key, (SEQS, TOKENS, HEADS, HD), 6.0)
    jitter = jax.random.uniform(jitter_key, (HEADS,), jnp.float32)
    spread = 10.0 ** (0.5 * (jnp.arange(HEADS).astype(jnp.float32) + jitter) / HEADS)
    return (base * spread[None, None, :, None]).reshape(SEQS, TOKENS, HID).astype(jnp.bfloat16)


def draw_grad_out(key, part):
    own_key = jax.random.fold_in(key, 29)
    base_key, jitter_key = jax.random.split(own_key, 2)
    base = rough_base(base_key, (SEQS, TOKENS, HID), 4.0)
    jitter = jax.random.uniform(jitter_key, (SEQS, TOKENS), jnp.float32)
    exponent = 0.7 * jnp.arange(TOKENS).astype(jnp.float32)[None, :] / TOKENS + 0.3 * jitter
    return (base * (0.3 * 10.0 ** exponent)[:, :, None]).astype(jnp.bfloat16)


def block_levels(rng, extent, shards, smallest, high):
    gain = 1.0
    for position, parts in shards:
        steps = jax.random.uniform(jax.random.fold_in(jax.random.fold_in(rng, 6), position), (parts,), jnp.float32, smallest / len(shards), high / len(shards))
        gain = gain * jnp.repeat(jnp.exp(steps), extent[position] // parts).reshape((-1,) + (1,) * (len(extent) - 1 - position))
    return gain


def noise(key, extent, width, limit, shards=(), dtype=jnp.bfloat16):
    array = width * jax.random.normal(key, extent, jnp.float32)
    if shards:
        array = array * block_levels(key, extent, shards, -0.22, 0.18)
    return jnp.clip(array, -limit, limit).astype(dtype)


def setup_inputs(seed: int = 0) -> dict:
    seeds = jax.random.split(jax.random.key(seed), 6)
    return {
        "queries": noise(seeds[0], (SEQS, TOKENS, HID), HD ** -0.5, 0.5, ((0, 2), (1, 4), (2, 4))),
        "keys": noise(seeds[1], (SEQS, TOKENS, HID), TOKENS ** -0.5, 0.25, ((0, 2), (1, 4), (2, 4))),
        "values": draw_values(jax.random.fold_in(seeds[5], 71), 0),
        "out_gain": jnp.clip(1.0 + 0.18 * jax.random.normal(seeds[3], (HID,), jnp.float32), 0.1, 1.9),
        "grad_out": draw_grad_out(jax.random.fold_in(seeds[5], 71), 0),
    }


EPSILON = 1e-06
MATMUL_PRECISION = lax.Precision.HIGHEST

def split_heads(matrix):
    return matrix.reshape(TOKENS // BLOCK, BLOCK, HEADS, HD).transpose(2, 0, 1, 3)

def join_heads(stacked):
    return stacked.transpose(1, 2, 0, 3).reshape(TOKENS, HID)

def causal_mask():
    return jnp.arange(BLOCK)[:, None] >= jnp.arange(BLOCK)[None, :]

def round_bf16(matrix):
    return lax.optimization_barrier(matrix.astype(jnp.bfloat16)).astype(jnp.float32)

def block_scores(query_matrix_rows, key_rows):
    attention_scores = jnp.einsum('nid,njd->nij', query_matrix_rows, key_rows, precision=MATMUL_PRECISION)
    return round_bf16(jnp.where(causal_mask(), attention_scores, 0.0))

def block_forward(items):
    query_matrix_rows = items[0].astype(jnp.float32)
    key_rows = items[1].astype(jnp.float32)
    value_matrix_rows = items[2].astype(jnp.float32)
    states = jnp.einsum('nbd,nbe->nde', key_rows, value_matrix_rows, precision=MATMUL_PRECISION)
    running = jnp.cumsum(states, axis=0)
    preceding_state_sum = jnp.concatenate([jnp.zeros_like(states[:1]), running[:-1]], axis=0)
    attention_scores = block_scores(query_matrix_rows, key_rows)
    attention_output = jnp.einsum('pqg,pgv->pqv', attention_scores, value_matrix_rows, precision=MATMUL_PRECISION)
    attention_output = attention_output + jnp.einsum('uag,ugl->ual', query_matrix_rows, preceding_state_sum, precision=MATMUL_PRECISION)
    return (attention_output, preceding_state_sum)

def block_backward(items):
    query_matrix_rows = items[0].astype(jnp.float32)
    key_rows = items[1].astype(jnp.float32)
    value_matrix_rows = items[2].astype(jnp.float32)
    upstream_gradient_rows = items[3].astype(jnp.float32)
    preceding_state_sum = items[4]
    block_parts = jnp.einsum('ykw,ykp->ywp', query_matrix_rows, upstream_gradient_rows, precision=MATMUL_PRECISION)
    running = jnp.cumsum(block_parts[::-1], axis=0)[::-1]
    later_sum = jnp.concatenate([running[1:], jnp.zeros_like(block_parts[:1])], axis=0)
    attention_scores = block_scores(query_matrix_rows, key_rows)
    combined_gradient = jnp.einsum('ozy,oly->ozl', upstream_gradient_rows, value_matrix_rows, precision=MATMUL_PRECISION)
    combined_gradient = round_bf16(jnp.where(causal_mask(), combined_gradient, 0.0))
    query_gradient = jnp.einsum('nij,njd->nid', combined_gradient, key_rows, precision=MATMUL_PRECISION)
    query_gradient = query_gradient + jnp.einsum('qbz,qmz->qbm', upstream_gradient_rows, preceding_state_sum, precision=MATMUL_PRECISION)
    grad_keys = jnp.einsum('nij,nid->njd', combined_gradient, query_matrix_rows, precision=MATMUL_PRECISION)
    grad_keys = grad_keys + jnp.einsum('nje,nde->njd', value_matrix_rows, later_sum, precision=MATMUL_PRECISION)
    value_gradient = jnp.einsum('lfa,lfz->laz', attention_scores, upstream_gradient_rows, precision=MATMUL_PRECISION)
    value_gradient = value_gradient + jnp.einsum('njd,nde->nje', key_rows, later_sum, precision=MATMUL_PRECISION)
    return (query_gradient, grad_keys, value_gradient)

def reference(queries, keys, values, out_gain, grad_out):

    def one_sequence(items):
        query_heads = split_heads(items[0])
        key_heads = split_heads(items[1])
        value_heads = split_heads(items[2])
        attention_output, preceding_state_sum = lax.map(block_forward, (query_heads, key_heads, value_heads))
        attention_output = join_heads(attention_output)
        gradient = items[3].astype(jnp.float32)
        rescale = lax.rsqrt(lax.optimization_barrier(jnp.sum(attention_output * attention_output, axis=1, keepdims=True)) / HID + EPSILON)
        normed = (attention_output * rescale * out_gain).astype(jnp.bfloat16)
        gain_part = lax.optimization_barrier(jnp.sum(gradient * attention_output * rescale, axis=0))
        crossed = lax.optimization_barrier(jnp.sum(gradient * out_gain * attention_output, axis=1, keepdims=True))
        upstream = out_gain * gradient * rescale - attention_output * (rescale * rescale * rescale) * crossed / HID
        upstream = lax.optimization_barrier(upstream.astype(jnp.bfloat16))
        grads = lax.map(block_backward, (query_heads, key_heads, value_heads, split_heads(upstream), preceding_state_sum))
        return (normed, join_heads(grads[0]).astype(jnp.bfloat16), join_heads(grads[1]).astype(jnp.bfloat16), join_heads(grads[2]).astype(jnp.bfloat16), gain_part)
    outputs = lax.map(one_sequence, (queries, keys, values, grad_out))
    return (outputs[0], outputs[1], outputs[2], outputs[3], lax.optimization_barrier(jnp.sum(outputs[4], axis=0)))
```

```python
import functools

import jax
import jax.numpy as jnp
from jax import lax
from jax.experimental import pallas as pl
from jax.experimental.pallas import tpu as pltpu
from jax.sharding import PartitionSpec as P

HD = 128
HID = 4096
EPSILON = 1e-06
PIECES = 4
PART = HD // PIECES
MESH = pl.DeviceIdType.MESH
F32 = jnp.float32
BF16 = jnp.bfloat16


def dot(a, b, ca, cb):
    return lax.dot_general(a, b, (((ca,), (cb,)), ((), ())), preferred_element_type=F32)


def split(x):
    high = x.astype(BF16)
    return high, (x - high.astype(F32)).astype(BF16)


def dot_wide(a, x, ca, cb):
    high, low = split(x)
    return dot(a, high, ca, cb) + dot(a, low, ca, cb)


def kernel(
    n_seq, n_tp, n_dp,
    q_in, k_in, v_in, gain_in, g_in,
    normed_out, dq_out, dk_out, dv_out, gg_out,
    q_ref, k_ref, v_ref, gain_ref, g_ref,
    prior, total, later, total_back,
    att, scores, mixed, squares, crossed, dk_part, dv_part, up, normed, dq, dk, dv,
    stat, gain_seq, gain_dp, gg, gain_back,
    in_sem, out_sem,
    up_send, up_recv, down_send, down_recv,
    stat_send, stat_recv, gs_send, gs_recv, gd_send, gd_recv,
    gb_send, gb_recv,
):
    rows, width = q_ref.shape
    heads = width // HD
    z = lax.axis_index("seq")
    t = lax.axis_index("tp")
    d = lax.axis_index("dp")
    first, last = z == 0, z == n_seq - 1
    above = lax.rem(z + 1, n_seq)
    below = lax.rem(z + n_seq - 1, n_seq)

    def head(h):
        return slice(h * HD, (h + 1) * HD)

    def peers(axis, me, size):
        return [{axis: lax.rem(me + i, size)} for i in range(1, size)]

    greeted = peers("tp", t, n_tp) + peers("dp", d, n_dp)
    if n_seq > 1:
        greeted.append({"seq": below})
    barrier = pltpu.get_barrier_semaphore()
    for peer in greeted:
        pl.semaphore_signal(barrier, inc=1, device_id=peer, device_id_type=MESH)

    loads = [
        pltpu.make_async_copy(src, dst, in_sem.at[i])
        for i, (src, dst) in enumerate(
            [(k_in, k_ref), (v_in, v_ref), (q_in, q_ref), (g_in, g_ref), (gain_in, gain_ref)]
        )
    ]
    for load in loads:
        load.start()
    loads[0].wait()
    loads[1].wait()

    def part(p):
        return slice(p * PART, (p + 1) * PART)

    def move_up(h, p):
        i = h * PIECES + p
        return pltpu.make_async_remote_copy(
            src_ref=total.at[h, part(p)], dst_ref=prior.at[h, part(p)],
            send_sem=up_send.at[i], recv_sem=up_recv.at[i],
            device_id={"seq": above}, device_id_type=MESH,
        )

    def move_down(h, p):
        i = h * PIECES + p
        return pltpu.make_async_remote_copy(
            src_ref=total_back.at[h, part(p)], dst_ref=later.at[h, part(p)],
            send_sem=down_send.at[i], recv_sem=down_recv.at[i],
            device_id={"seq": below}, device_id_type=MESH,
        )

    def relay(h, p, mine, come, move, is_first, is_last):
        @pl.when(jnp.logical_and(jnp.logical_not(is_first), jnp.logical_not(is_last)))
        def _():
            move(h, p).wait_recv()
            mine[h, part(p)] = mine[h, part(p)] + come[h, part(p)]
            move(h, p).start()

        @pl.when(jnp.logical_and(is_last, jnp.logical_not(is_first)))
        def _():
            move(h, p).wait_recv()

    def relay_all(mine, come, move, is_first, is_last, slots):
        for h in range(heads):
            for p in range(PIECES):
                relay(h, p, mine, come, move, is_first, is_last)
                for step in slots[h * PIECES + p]:
                    step()

    for h in range(heads):
        total[h] = dot(k_ref[:, head(h)], v_ref[:, head(h)], 0, 0)
        if h == 0:
            pl.semaphore_wait(barrier, len(greeted))
        if n_seq > 1:
            @pl.when(first)
            def _():
                for p in range(PIECES):
                    move_up(h, p).start()

    @pl.when(first)
    def _():
        prior[...] = jnp.zeros_like(prior)

    @pl.when(last)
    def _():
        later[...] = jnp.zeros_like(later)

    loads[2].wait()
    loads[3].wait()
    loads[4].wait()
    causal = lax.broadcasted_iota(jnp.int32, (rows, rows), 0) >= lax.broadcasted_iota(
        jnp.int32, (rows, rows), 1
    )
    def score_of(h):
        score = jnp.where(causal, dot(q_ref[:, head(h)], k_ref[:, head(h)], 1, 1), 0.0)
        scores[h] = score.astype(BF16)

    def attend_block(h):
        att[:, head(h)] = dot(scores[h], v_ref[:, head(h)], 1, 0)

    def attend_prior(h):
        att[:, head(h)] = att[:, head(h)] + dot_wide(q_ref[:, head(h)], prior[h], 1, 0)

    def add_stats(h):
        out = att[:, head(h)]
        square = out * out
        cross = g_ref[:, head(h)].astype(F32) * gain_ref[h:h + 1, :] * out
        squares[...] = square if h == 0 else squares[...] + square
        crossed[...] = cross if h == 0 else crossed[...] + cross

    slots = [[] for _ in range(heads * PIECES)]
    for h in range(heads):
        slots[h * PIECES].append(functools.partial(score_of, h))
        slots[h * PIECES + 1].append(functools.partial(attend_block, h))
        if h > 0:
            slots[h * PIECES + 2].append(functools.partial(attend_prior, h - 1))
            slots[h * PIECES + 3].append(functools.partial(add_stats, h - 1))
    relay_all(total, prior, move_up, first, last, slots)
    attend_prior(heads - 1)
    add_stats(heads - 1)

    stat[t, 0:1, :] = jnp.sum(squares[...].T, axis=0, keepdims=True)
    stat[t, 1:2, :] = jnp.sum(crossed[...].T, axis=0, keepdims=True)

    def all_send(buffer, axis, me, size, send, recv):
        return [
            pltpu.make_async_remote_copy(
                src_ref=buffer.at[me], dst_ref=buffer.at[me],
                send_sem=send.at[i - 1], recv_sem=recv.at[i - 1],
                device_id={axis: lax.rem(me + i, size)}, device_id_type=MESH,
            )
            for i in range(1, size)
        ]

    stat_moves = all_send(stat, "tp", t, n_tp, stat_send, stat_recv)
    for move in stat_moves:
        move.start()
    for move in stat_moves:
        move.wait_recv()
    sums = stat[0, 0:2, :]
    for i in range(1, n_tp):
        sums = sums + stat[i, 0:2, :]
    scale_row = lax.rsqrt(sums[0:1] / HID + EPSILON)
    factor_row = scale_row * scale_row * scale_row * sums[1:2] / HID
    scale = jnp.broadcast_to(scale_row, (HD, rows)).T
    factor = jnp.broadcast_to(factor_row, (HD, rows)).T

    def upstream(h):
        out = att[:, head(h)]
        grad = g_ref[:, head(h)].astype(F32)
        scaled = grad * scale
        up[:, head(h)] = (gain_ref[h:h + 1, :] * scaled - out * factor).astype(BF16)
        gain_seq[z, h:h + 1, :] = jnp.sum(scaled * out, axis=0, keepdims=True)

    def back_state(h):
        total_back[h] = dot(q_ref[:, head(h)], up[:, head(h)], 0, 0)
        if n_seq > 1:
            @pl.when(last)
            def _():
                for p in range(PIECES):
                    move_down(h, p).start()

    upstream(0)
    back_state(0)
    for h in range(1, heads):
        upstream(h)

    def gain_to_first(source):
        return pltpu.make_async_remote_copy(
            src_ref=gain_seq.at[source], dst_ref=gain_seq.at[source],
            send_sem=gs_send.at[source], recv_sem=gs_recv.at[source],
            device_id={"seq": 0}, device_id_type=MESH,
        )

    def gain_from_first(target):
        return pltpu.make_async_remote_copy(
            src_ref=gg, dst_ref=gain_back,
            send_sem=gb_send.at[target], recv_sem=gb_recv.at[target],
            device_id={"seq": target}, device_id_type=MESH,
        )

    @pl.when(jnp.logical_not(first))
    def _():
        gain_to_first(z).start()

    for h in range(1, heads):
        back_state(h)

    dp_moves = all_send(gain_dp, "dp", d, n_dp, gd_send, gd_recv)
    stores = []

    def store(src, dst):
        copy = pltpu.make_async_copy(src, dst, out_sem.at[len(stores)])
        copy.start()
        stores.append(copy)

    def normed_of(h):
        normed[:, head(h)] = (att[:, head(h)] * scale * gain_ref[h:h + 1, :]).astype(BF16)
        store(normed.at[:, head(h)], normed_out.at[:, head(h)])

    def mixed_of(h):
        mix = jnp.where(causal, dot(up[:, head(h)], v_ref[:, head(h)], 1, 1), 0.0)
        mixed[h] = mix.astype(BF16)

    def dq_of(h):
        dq[:, head(h)] = (
            dot(mixed[h], k_ref[:, head(h)], 1, 0) + dot_wide(up[:, head(h)], prior[h], 1, 1)
        ).astype(BF16)
        store(dq.at[:, head(h)], dq_out.at[:, head(h)])

    def block_parts(h):
        dk_part[h] = dot(mixed[h], q_ref[:, head(h)], 0, 0)
        dv_part[h] = dot(scores[h], up[:, head(h)], 0, 0)

    def dk_of(h):
        wide = dot_wide(v_ref[:, head(h)], later[h], 1, 1)
        dk[:, head(h)] = (dk_part[h] + wide).astype(BF16)
        store(dk.at[:, head(h)], dk_out.at[:, head(h)])

    def dv_of(h):
        wide = dot_wide(k_ref[:, head(h)], later[h], 1, 0)
        dv[:, head(h)] = (dv_part[h] + wide).astype(BF16)
        store(dv.at[:, head(h)], dv_out.at[:, head(h)])

    def gain_middle():
        @pl.when(first)
        def _():
            for source in range(1, n_seq):
                gain_to_first(source).wait_recv()
            gain_sum = gain_seq[0]
            for i in range(1, n_seq):
                gain_sum = gain_sum + gain_seq[i]
            gain_dp[d] = gain_sum
            for move in dp_moves:
                move.start()

    def gain_end():
        @pl.when(first)
        def _():
            for move in dp_moves:
                move.wait_recv()
            gain_sum = gain_dp[0]
            for i in range(1, n_dp):
                gain_sum = gain_sum + gain_dp[i]
            gg[...] = gain_sum
            for target in range(1, n_seq):
                gain_from_first(target).start()

    block_work = [
        functools.partial(work, h)
        for h in range(heads)
        for work in (mixed_of, dq_of, block_parts, normed_of)
    ]
    half = 2 * heads
    for step in block_work[:half]:
        step()
    slots = [[] for _ in range(heads * PIECES)]
    for h in range(heads):
        if h > 0:
            slots[h * PIECES].append(functools.partial(dk_of, h - 1))
            slots[h * PIECES + 1].append(functools.partial(dv_of, h - 1))
        slots[h * PIECES + 2].append(block_work[half + 2 * h])
        slots[h * PIECES + 3].append(block_work[half + 2 * h + 1])
    slots[0].append(gain_middle)
    slots[heads // 4 * PIECES].append(gain_end)
    relay_all(total_back, later, move_down, last, first, slots)
    dk_of(heads - 1)
    dv_of(heads - 1)

    gg_copy = pltpu.make_async_copy(gg, gg_out, out_sem.at[4 * heads])

    @pl.when(first)
    def _():
        gg_copy.start()
        for move in dp_moves:
            move.wait_send()
        for target in range(1, n_seq):
            gain_from_first(target).wait_send()

    back_copy = pltpu.make_async_copy(gain_back, gg_out, out_sem.at[4 * heads])

    @pl.when(jnp.logical_not(first))
    def _():
        gain_from_first(z).wait_recv()
        back_copy.start()
        gain_to_first(z).wait_send()

    for move in stat_moves:
        move.wait_send()
    if n_seq > 1:
        @pl.when(jnp.logical_not(last))
        def _():
            for h in range(heads):
                for p in range(PIECES):
                    move_up(h, p).wait_send()

        @pl.when(jnp.logical_not(first))
        def _():
            for h in range(heads):
                for p in range(PIECES):
                    move_down(h, p).wait_send()
    for copy in stores:
        copy.wait()

    @pl.when(first)
    def _():
        gg_copy.wait()

    @pl.when(jnp.logical_not(first))
    def _():
        back_copy.wait()


def helped(
    n_tp, n_dp,
    q_in, k_in, v_in, gain_in, g_in,
    normed_out, dq_out, dk_out, dv_out, gg_out,
    q_ref, k_ref, v_ref, gain_ref, g_ref,
    prior, total, later, total_back,
    att, scores, mixed, squares, crossed, dk_part, dv_part, up, normed, dq, dk, dv,
    early_out, early_in, help_att,
    stat, gain_seq, gain_dp, gg, gain_back,
    in_sem, out_sem,
    up_send, up_recv, down_send, down_recv,
    early_send, early_recv,
    stat_send, stat_recv, gs_send, gs_recv, gd_send, gd_recv,
    gb_send, gb_recv,
):
    rows, width = q_ref.shape
    heads = width // HD
    far, near, common = heads - 1, (heads - 3, heads - 2), tuple(range(heads - 3))
    z = lax.axis_index("seq")
    t = lax.axis_index("tp")
    d = lax.axis_index("dp")
    slot = z * n_tp + t

    def head(h):
        return slice(h * HD, (h + 1) * HD)

    def part(p):
        return slice(p * PART, (p + 1) * PART)

    def tp_peer(i):
        return lax.rem(t + i, n_tp)

    causal = lax.broadcasted_iota(jnp.int32, (rows, rows), 0) >= lax.broadcasted_iota(
        jnp.int32, (rows, rows), 1
    )
    loads = [
        pltpu.make_async_copy(src, dst, in_sem.at[i])
        for i, (src, dst) in enumerate(
            [(k_in, k_ref), (v_in, v_ref), (q_in, q_ref), (g_in, g_ref), (gain_in, gain_ref)]
        )
    ]

    def program(own):
        barrier = pltpu.get_barrier_semaphore()
        greeted = [{"tp": tp_peer(i)} for i in range(1, n_tp)]
        heard = len(greeted)
        if own == 0:
            greeted += [{"dp": lax.rem(d + i, n_dp)} for i in range(1, n_dp)]
            heard = len(greeted) + 1
        else:
            heard += 2
        greeted += [{"seq": i} for i in ((1,), (0, 2, 3), (1, 3), (2,))[own]]
        for peer in greeted:
            pl.semaphore_signal(barrier, inc=1, device_id=peer, device_id_type=MESH)
        for load in loads:
            load.start()

        stores, sent = [], []

        def send(move):
            move.start()
            sent.append(move)

        def store(src, dst):
            copy = pltpu.make_async_copy(src, dst, out_sem.at[len(stores)])
            copy.start()
            stores.append(copy)

        def move_up(h, p):
            i = h * PIECES + p
            return pltpu.make_async_remote_copy(
                src_ref=total.at[h, part(p)], dst_ref=prior.at[h, part(p)],
                send_sem=up_send.at[i], recv_sem=up_recv.at[i],
                device_id={"seq": min(own + 1, 3)}, device_id_type=MESH,
            )

        def move_down(h, p):
            i = h * PIECES + p
            return pltpu.make_async_remote_copy(
                src_ref=total_back.at[h, part(p)], dst_ref=later.at[h, part(p)],
                send_sem=down_send.at[i], recv_sem=down_recv.at[i],
                device_id={"seq": max(own - 1, 0)}, device_id_type=MESH,
            )

        def arrive(move, h):
            for p in range(PIECES):
                move(h, p).wait_recv()

        def move_early(i, j, target):
            return pltpu.make_async_remote_copy(
                src_ref=early_out.at[i], dst_ref=early_in.at[j],
                send_sem=early_send.at[i], recv_sem=early_recv.at[j],
                device_id={"seq": target}, device_id_type=MESH,
            )

        def early_arrive(j):
            move_early(0, j, own - 1).wait_recv()

        def total_of(h):
            total[h] = dot(k_ref[:, head(h)], v_ref[:, head(h)], 0, 0)

        def score_of(h):
            score = jnp.where(causal, dot(q_ref[:, head(h)], k_ref[:, head(h)], 1, 1), 0.0)
            scores[h] = score.astype(BF16)

        def attend_block(h):
            att[:, head(h)] = dot(scores[h], v_ref[:, head(h)], 1, 0)

        def attend_prior(h):
            att[:, head(h)] = att[:, head(h)] + dot_wide(q_ref[:, head(h)], prior[h], 1, 0)

        counted = set()

        def count(i, out, weighted):
            square, cross = out * out, weighted * out
            squares[i] = squares[i] + square if i in counted else square
            crossed[i] = crossed[i] + cross if i in counted else cross
            counted.add(i)

        def add_stats(h):
            count(0, att[:, head(h)], g_ref[:, head(h)].astype(F32) * gain_ref[h:h + 1, :])

        def send_early(h, first, slots, target):
            early_out[first] = q_ref[:, head(h)].astype(F32)
            send(move_early(first, slots, target))
            early_out[first + 1] = g_ref[:, head(h)].astype(F32)
            send(move_early(first + 1, slots + 1, target))
            score_of(h)
            local = dot(scores[h], v_ref[:, head(h)], 1, 0)
            att[:, head(h)] = local
            early_out[first + 2] = local
            send(move_early(first + 2, slots + 2, target))

        def help_attend(j, first, h, state, i):
            out = early_in[first + 2] + dot_wide(early_in[first].astype(BF16), state, 1, 0)
            help_att[j] = out
            count(i, out, early_in[first + 1] * gain_ref[h:h + 1, :])

        def help_back(j, first, h, factors):
            scaled = early_in[first + 1] * factors[0]
            grad = (gain_ref[h:h + 1, :] * scaled - help_att[j] * factors[1]).astype(BF16)
            return dot(early_in[first].astype(BF16), grad, 0, 0)

        def relay(mine, come, move, order, slots, start=True):
            slots = list(slots)
            for h in order:
                for p in range(PIECES):
                    move(h, p).wait_recv()
                    mine[h, part(p)] = mine[h, part(p)] + come[h, part(p)]
                    send(move(h, p))
                    if slots:
                        slots.pop(0)()
            for step in slots:
                step()

        def put_stats():
            for i in sorted(counted):
                b = 2 * (own + i)
                stat[slot, b:b + 1, :] = jnp.sum(squares[i].T, axis=0, keepdims=True)
                stat[slot, b + 1:b + 2, :] = jnp.sum(crossed[i].T, axis=0, keepdims=True)

        def stat_move(n, target, i):
            return pltpu.make_async_remote_copy(
                src_ref=stat.at[slot], dst_ref=stat.at[slot],
                send_sem=stat_send.at[n], recv_sem=stat_recv.at[slot],
                device_id={"seq": target, "tp": tp_peer(i)}, device_id_type=MESH,
            )

        def send_stats():
            n = 0
            for target in ((0,), (1, 3, 2), (2, 3, 1), (3, 2, 1))[own]:
                for i in range(1 if target == own else 0, n_tp):
                    send(stat_move(n, target, i))
                    n += 1

        def sum_stats(source):
            for i in range(1 if source == own else 0, n_tp):
                s = source * n_tp + tp_peer(i)
                pltpu.make_async_remote_copy(
                    src_ref=stat.at[s], dst_ref=stat.at[s],
                    send_sem=stat_send.at[0], recv_sem=stat_recv.at[s],
                    device_id={"tp": tp_peer(1)}, device_id_type=MESH,
                ).wait_recv()
            total_stat = stat[source * n_tp]
            for i in range(1, n_tp):
                total_stat = total_stat + stat[source * n_tp + i]
            return total_stat

        def factors_of(sums, b):
            scale = lax.rsqrt(sums[2 * b:2 * b + 1] / HID + EPSILON)
            factor = scale * scale * scale * sums[2 * b + 1:2 * b + 2] / HID
            return tuple(jnp.broadcast_to(x, (HD, rows)).T for x in (scale, factor))

        def upstream(h, factors):
            out = att[:, head(h)]
            scaled = g_ref[:, head(h)].astype(F32) * factors[0]
            up[:, head(h)] = (gain_ref[h:h + 1, :] * scaled - out * factors[1]).astype(BF16)
            gain_seq[own, h:h + 1, :] = jnp.sum(scaled * out, axis=0, keepdims=True)

        def back_state(h):
            total_back[h] = dot(q_ref[:, head(h)], up[:, head(h)], 0, 0)

        def send_down(h):
            for p in range(PIECES):
                send(move_down(h, p))

        def gain_to_first(source):
            return pltpu.make_async_remote_copy(
                src_ref=gain_seq.at[source], dst_ref=gain_seq.at[source],
                send_sem=gs_send.at[source], recv_sem=gs_recv.at[source],
                device_id={"seq": 0}, device_id_type=MESH,
            )

        def gain_from_first(target):
            return pltpu.make_async_remote_copy(
                src_ref=gg, dst_ref=gain_back,
                send_sem=gb_send.at[target], recv_sem=gb_recv.at[target],
                device_id={"seq": target}, device_id_type=MESH,
            )

        def normed_of(h, factors):
            normed[:, head(h)] = (
                att[:, head(h)] * factors[0] * gain_ref[h:h + 1, :]
            ).astype(BF16)
            store(normed.at[:, head(h)], normed_out.at[:, head(h)])

        def mixed_of(h):
            mix = jnp.where(causal, dot(up[:, head(h)], v_ref[:, head(h)], 1, 1), 0.0)
            mixed[h] = mix.astype(BF16)

        def dq_of(h):
            wide = dot(mixed[h], k_ref[:, head(h)], 1, 0)
            if own > 0:
                wide = wide + dot_wide(up[:, head(h)], prior[h], 1, 1)
            dq[:, head(h)] = wide.astype(BF16)
            store(dq.at[:, head(h)], dq_out.at[:, head(h)])

        def block_parts(h):
            dk_part[h] = dot(mixed[h], q_ref[:, head(h)], 0, 0)
            dv_part[h] = dot(scores[h], up[:, head(h)], 0, 0)

        def dk_of(h):
            wide = dk_part[h]
            if own < 3:
                wide = wide + dot_wide(v_ref[:, head(h)], later[h], 1, 1)
            dk[:, head(h)] = wide.astype(BF16)
            store(dk.at[:, head(h)], dk_out.at[:, head(h)])

        def dv_of(h):
            wide = dv_part[h]
            if own < 3:
                wide = wide + dot_wide(k_ref[:, head(h)], later[h], 1, 0)
            dv[:, head(h)] = wide.astype(BF16)
            store(dv.at[:, head(h)], dv_out.at[:, head(h)])

        def local_work(h, factors):
            return [
                functools.partial(mixed_of, h),
                functools.partial(dq_of, h),
                functools.partial(block_parts, h),
                functools.partial(normed_of, h, factors),
            ]

        def last_work(h):
            return [functools.partial(dk_of, h), functools.partial(dv_of, h)]

        def run(steps):
            for step in steps:
                step()

        def forward_slots(order, extra):
            slots, held = [], []
            for h in order:
                slots += [functools.partial(score_of, h), functools.partial(attend_block, h)]
                slots += held if held else [lambda: None] * 2
                held = extra(h)
            return slots + held

        stat[slot] = jnp.zeros_like(stat[slot])
        for load in loads:
            load.wait()

        if own == 0:
            for h in range(heads):
                total_of(h)
                if h == 0:
                    pl.semaphore_wait(barrier, heard)
                for p in range(PIECES):
                    send(move_up(h, p))
            for h in range(heads):
                score_of(h)
                attend_block(h)
                add_stats(h)
            put_stats()
            send_stats()
            factors = factors_of(sum_stats(0), 0)
            for h in range(heads):
                upstream(h, factors)
            for h in range(heads):
                run(local_work(h, factors))
            gains = [{"dp": lax.rem(d + i, n_dp)} for i in range(1, n_dp)]
            gain_moves = [
                pltpu.make_async_remote_copy(
                    src_ref=gain_dp.at[d], dst_ref=gain_dp.at[d],
                    send_sem=gd_send.at[i], recv_sem=gd_recv.at[i],
                    device_id=peer, device_id_type=MESH,
                )
                for i, peer in enumerate(gains)
            ]
            order = (far,) + near + common
            for n, h in enumerate(order):
                arrive(move_down, h)
                run(last_work(h))
                if n == 3:
                    for source in range(1, 4):
                        gain_to_first(source).wait_recv()
                    gain_dp[d] = (gain_seq[0] + gain_seq[1]) + (gain_seq[2] + gain_seq[3])
                    for move in gain_moves:
                        send(move)
                if n == 5:
                    for move in gain_moves:
                        move.wait_recv()
                    gain_sum = gain_dp[0]
                    for i in range(1, n_dp):
                        gain_sum = gain_sum + gain_dp[i]
                    gg[...] = gain_sum
                    for target in range(1, 4):
                        send(gain_from_first(target))
                    store(gg, gg_out)

        if own == 1:
            pl.semaphore_wait(barrier, heard)
            for h in range(heads):
                total_of(h)
            relay(total, prior, move_up, range(heads), forward_slots(
                range(heads),
                lambda h: [functools.partial(attend_prior, h), functools.partial(add_stats, h)],
            ))
            for j in range(7):
                early_arrive(j)
            help_attend(0, 3, far, total[far], 1)
            help_attend(1, 0, far, total[far] + early_in[6], 2)
            put_stats()
            send_stats()
            sums = sum_stats(1)
            factors = factors_of(sums, 1)
            for h in (far,) + near + common:
                upstream(h, factors)
                back_state(h)
            send(gain_to_first(own))
            sums = sums + sum_stats(2)
            beyond = help_back(0, 3, far, factors_of(sums, 2))
            sums = sums + sum_stats(3)
            beyond = beyond + help_back(1, 0, far, factors_of(sums, 3))
            later[far] = beyond
            total_back[far] = total_back[far] + beyond
            send_down(far)
            steps = local_work(far, factors) + last_work(far)
            for h in near + common:
                steps += local_work(h, factors)
            run(steps[:10])
            slots = steps[10:]
            relay(total_back, later, move_down, near + common, slots)
            for h in near + common:
                run(last_work(h))

        if own == 2:
            total_of(far)
            pl.semaphore_wait(barrier, heard)
            early_out[3] = total[far]
            send(move_early(3, 6, 1))
            send_early(far, 0, 3, 1)
            for h in range(heads - 1):
                total_of(h)

            score_of(near[1])
            attend_block(near[1])

            def help_first():
                for j in range(3):
                    early_arrive(j)
                help_attend(0, 0, near[0], total[near[0]], 1)

            def own_part(h):
                return [functools.partial(attend_prior, h), functools.partial(add_stats, h)]

            slots = forward_slots(common + near[:1], own_part) + [help_first]
            relay(total, prior, move_up, range(heads - 1), slots)
            run(own_part(near[1]))
            for j in range(3, 6):
                early_arrive(j)
            help_attend(1, 3, near[1], total[near[1]], 1)
            put_stats()
            send_stats()
            relay(total, prior, move_up, (far,), ())
            attend_prior(far)
            sums = sum_stats(1) + sum_stats(2)
            factors = factors_of(sums, 2)
            for h in near:
                upstream(h, factors)
                back_state(h)
            sums = sums + sum_stats(3)
            ahead = factors_of(sums, 3)
            for j, h in enumerate(near):
                beyond = help_back(j, 3 * j, h, ahead)
                later[h] = beyond
                total_back[h] = total_back[h] + beyond
                send_down(h)
            for h in common:
                upstream(h, factors)
                back_state(h)
            upstream(far, factors)
            send(gain_to_first(own))
            steps = []
            for h in near:
                steps += local_work(h, factors) + last_work(h)
            for h in common + (far,):
                steps += local_work(h, factors)
            relay(total_back, later, move_down, common, steps)
            for h in common:
                run(last_work(h))
            arrive(move_down, far)
            run(last_work(far))

        if own == 3:
            pl.semaphore_wait(barrier, heard)
            send_early(far, 0, 0, 1)
            send_early(near[0], 3, 0, 2)
            send_early(near[1], 6, 3, 2)
            for h in common:
                score_of(h)
                attend_block(h)
            for h in common:
                arrive(move_up, h)
                attend_prior(h)
                add_stats(h)
            put_stats()
            send_stats()
            arrive(move_up, near[0])
            attend_prior(near[0])
            sums = sum_stats(1) + sum_stats(2)
            sums = sums + sum_stats(3)
            factors = factors_of(sums, 3)
            for h in common:
                upstream(h, factors)
                back_state(h)
                send_down(h)
            arrive(move_up, near[1])
            attend_prior(near[1])
            arrive(move_up, far)
            attend_prior(far)
            upstream(far, factors)
            back_state(far)
            send_down(far)
            for h in near:
                upstream(h, factors)
            send(gain_to_first(own))
            for h in range(heads):
                run(local_work(h, factors))
                run(last_work(h))

        if own > 0:
            gain_from_first(own).wait_recv()
            store(gain_back, gg_out)
        for move in sent:
            move.wait_send()
        for copy in stores:
            copy.wait()

    for own in range(4):
        pl.when(z == own)(functools.partial(program, own))


def write_out(*refs):
    copies = [pltpu.make_async_copy(refs[i], refs[5 + i], refs[10].at[i]) for i in range(5)]
    for copy in copies:
        copy.start()
    for copy in copies:
        copy.wait()


def solution(mesh):
    n_seq, n_tp, n_dp = (mesh.shape[name] for name in ("seq", "tp", "dp"))

    def local(queries, keys, values, out_gain, grad_out):
        shape = queries.shape
        rows, width = shape[0] * shape[1], shape[2]
        heads = width // HD
        chunks = heads * PIECES
        matrix = jax.ShapeDtypeStruct((rows, width), BF16)
        state = pltpu.VMEM((heads, HD, HD), F32)
        page = pltpu.VMEM((rows, width), BF16)
        tile = lambda *lead: pltpu.VMEM((*lead, rows, HD), F32)
        sems = pltpu.SemaphoreType.DMA
        flat = lambda x: x.reshape(rows, width)
        with_help = n_seq == 4 and rows == HD and heads >= 4
        if with_help:
            body = functools.partial(helped, n_tp, n_dp)
            sums, stats = tile(3), n_seq * n_tp
            early = [tile(9), tile(7), tile(2)]
            early_sems = [sems((9,)), sems((7,))]
            stat_sems = [sems((3 * n_tp,)), sems((n_seq * n_tp,))]
        else:
            body = functools.partial(kernel, n_seq, n_tp, n_dp)
            sums, stats, early, early_sems = tile(), n_tp, [], []
            stat_sems = [sems((max(n_tp - 1, 1),)), sems((max(n_tp - 1, 1),))]
        outs = pl.pallas_call(
            body,
            out_shape=(matrix,) * 4 + (jax.ShapeDtypeStruct((heads, HD), F32),),
            in_specs=[pl.BlockSpec(memory_space=pltpu.HBM)] * 5,
            out_specs=[pl.BlockSpec(memory_space=pl.ANY)] * 5,
            scratch_shapes=[
                page, page, page, pltpu.VMEM((heads, HD), F32), page,
                state, state, state, state,
                pltpu.VMEM((rows, width), F32),
                pltpu.VMEM((heads, rows, rows), BF16), pltpu.VMEM((heads, rows, rows), BF16),
                sums, sums, tile(heads), tile(heads),
                page, page, page, page, page,
                *early,
                pltpu.VMEM((stats, 8, rows), F32),
                pltpu.VMEM((n_seq, heads, HD), F32),
                pltpu.VMEM((n_dp, heads, HD), F32),
                pltpu.VMEM((heads, HD), F32), pltpu.VMEM((heads, HD), F32),
                sems((5,)), sems((4 * heads + 1,)),
                sems((chunks,)), sems((chunks,)), sems((chunks,)), sems((chunks,)),
                *early_sems,
                *stat_sems,
                sems((n_seq,)), sems((n_seq,)),
                sems((max(n_dp - 1, 1),)), sems((max(n_dp - 1, 1),)),
                sems((n_seq,)), sems((n_seq,)),
            ],
            compiler_params=pltpu.CompilerParams(
                collective_id=0, has_side_effects=True, vmem_limit_bytes=32 << 20
            ),
        )(
            *(
                pltpu.with_memory_space_constraint(x, pltpu.HBM)
                for x in (
                    flat(queries), flat(keys), flat(values),
                    out_gain.reshape(heads, HD), flat(grad_out),
                )
            )
        )
        outs = pl.pallas_call(
            write_out,
            out_shape=tuple(jax.ShapeDtypeStruct(x.shape, x.dtype) for x in outs),
            in_specs=[pl.BlockSpec(memory_space=pl.ANY)] * 5,
            out_specs=[pl.BlockSpec(memory_space=pl.ANY)] * 5,
            scratch_shapes=[sems((5,))],
            compiler_params=pltpu.CompilerParams(vmem_limit_bytes=8 << 20),
        )(*outs)
        return tuple(x.reshape(shape) for x in outs[:4]) + (outs[4].reshape(width),)

    spec = P("dp", "seq", "tp")
    return jax.shard_map(
        local,
        mesh=mesh,
        in_specs=(spec, spec, spec, P("tp"), spec),
        out_specs=(spec, spec, spec, spec, P("tp")),
        check_vma=False,
    )
```

```python
import functools

import jax
import jax.numpy as jnp
from jax import lax
from jax.experimental import pallas as pl
from jax.experimental.pallas import tpu as pltpu
from jax.sharding import PartitionSpec as P

HD = 128
HID = 4096
EPSILON = 1e-06
PIECES = 4
PART = HD // PIECES
MESH = pl.DeviceIdType.MESH
F32 = jnp.float32
BF16 = jnp.bfloat16


def dot(a, b, ca, cb):
    return lax.dot_general(a, b, (((ca,), (cb,)), ((), ())), preferred_element_type=F32)


def split(x):
    high = x.astype(BF16)
    return high, (x - high.astype(F32)).astype(BF16)


def dot_wide(a, x, ca, cb):
    high, low = split(x)
    return dot(a, high, ca, cb) + dot(a, low, ca, cb)


def kernel(
    n_seq, n_tp, n_dp,
    q_in, k_in, v_in, gain_in, g_in,
    normed_out, dq_out, dk_out, dv_out, gg_out,
    q_ref, k_ref, v_ref, gain_ref, g_ref,
    prior, total, later, total_back,
    att, scores, mixed, squares, crossed, dk_part, dv_part, up, normed, dq, dk, dv,
    stat, gain_seq, gain_dp, gg, gain_back,
    in_sem, out_sem,
    up_send, up_recv, down_send, down_recv,
    stat_send, stat_recv, gs_send, gs_recv, gd_send, gd_recv,
    gb_send, gb_recv,
):
    rows, width = q_ref.shape
    heads = width // HD
    z = lax.axis_index("seq")
    t = lax.axis_index("tp")
    d = lax.axis_index("dp")
    first, last = z == 0, z == n_seq - 1
    above = lax.rem(z + 1, n_seq)
    below = lax.rem(z + n_seq - 1, n_seq)

    def head(h):
        return slice(h * HD, (h + 1) * HD)

    def peers(axis, me, size):
        return [{axis: lax.rem(me + i, size)} for i in range(1, size)]

    greeted = peers("tp", t, n_tp) + peers("dp", d, n_dp)
    if n_seq > 1:
        greeted.append({"seq": below})
    barrier = pltpu.get_barrier_semaphore()
    for peer in greeted:
        pl.semaphore_signal(barrier, inc=1, device_id=peer, device_id_type=MESH)

    loads = [
        pltpu.make_async_copy(src, dst, in_sem.at[i])
        for i, (src, dst) in enumerate(
            [(k_in, k_ref), (v_in, v_ref), (q_in, q_ref), (g_in, g_ref), (gain_in, gain_ref)]
        )
    ]
    for load in loads:
        load.start()
    loads[0].wait()
    loads[1].wait()

    def part(p):
        return slice(p * PART, (p + 1) * PART)

    def move_up(h, p):
        i = h * PIECES + p
        return pltpu.make_async_remote_copy(
            src_ref=total.at[h, part(p)], dst_ref=prior.at[h, part(p)],
            send_sem=up_send.at[i], recv_sem=up_recv.at[i],
            device_id={"seq": above}, device_id_type=MESH,
        )

    def move_down(h, p):
        i = h * PIECES + p
        return pltpu.make_async_remote_copy(
            src_ref=total_back.at[h, part(p)], dst_ref=later.at[h, part(p)],
            send_sem=down_send.at[i], recv_sem=down_recv.at[i],
            device_id={"seq": below}, device_id_type=MESH,
        )

    def relay(h, p, mine, come, move, is_first, is_last):
        @pl.when(jnp.logical_and(jnp.logical_not(is_first), jnp.logical_not(is_last)))
        def _():
            move(h, p).wait_recv()
            mine[h, part(p)] = mine[h, part(p)] + come[h, part(p)]
            move(h, p).start()

        @pl.when(jnp.logical_and(is_last, jnp.logical_not(is_first)))
        def _():
            move(h, p).wait_recv()

    def relay_all(mine, come, move, is_first, is_last, slots):
        for h in range(heads):
            for p in range(PIECES):
                relay(h, p, mine, come, move, is_first, is_last)
                for step in slots[h * PIECES + p]:
                    step()

    for h in range(heads):
        total[h] = dot(k_ref[:, head(h)], v_ref[:, head(h)], 0, 0)
        if h == 0:
            pl.semaphore_wait(barrier, len(greeted))
        if n_seq > 1:
            @pl.when(first)
            def _():
                for p in range(PIECES):
                    move_up(h, p).start()

    @pl.when(first)
    def _():
        prior[...] = jnp.zeros_like(prior)

    @pl.when(last)
    def _():
        later[...] = jnp.zeros_like(later)

    loads[2].wait()
    loads[3].wait()
    loads[4].wait()
    causal = lax.broadcasted_iota(jnp.int32, (rows, rows), 0) >= lax.broadcasted_iota(
        jnp.int32, (rows, rows), 1
    )
    def score_of(h):
        score = jnp.where(causal, dot(q_ref[:, head(h)], k_ref[:, head(h)], 1, 1), 0.0)
        scores[h] = score.astype(BF16)

    def attend_block(h):
        att[:, head(h)] = dot(scores[h], v_ref[:, head(h)], 1, 0)

    def attend_prior(h):
        att[:, head(h)] = att[:, head(h)] + dot_wide(q_ref[:, head(h)], prior[h], 1, 0)

    def add_stats(h):
        out = att[:, head(h)]
        square = out * out
        cross = g_ref[:, head(h)].astype(F32) * gain_ref[h:h + 1, :] * out
        squares[...] = square if h == 0 else squares[...] + square
        crossed[...] = cross if h == 0 else crossed[...] + cross

    slots = [[] for _ in range(heads * PIECES)]
    for h in range(heads):
        slots[h * PIECES].append(functools.partial(score_of, h))
        slots[h * PIECES + 1].append(functools.partial(attend_block, h))
        if h > 0:
            slots[h * PIECES + 2].append(functools.partial(attend_prior, h - 1))
            slots[h * PIECES + 3].append(functools.partial(add_stats, h - 1))
    relay_all(total, prior, move_up, first, last, slots)
    attend_prior(heads - 1)
    add_stats(heads - 1)

    stat[t, 0:1, :] = jnp.sum(squares[...].T, axis=0, keepdims=True)
    stat[t, 1:2, :] = jnp.sum(crossed[...].T, axis=0, keepdims=True)

    def all_send(buffer, axis, me, size, send, recv):
        return [
            pltpu.make_async_remote_copy(
                src_ref=buffer.at[me], dst_ref=buffer.at[me],
                send_sem=send.at[i - 1], recv_sem=recv.at[i - 1],
                device_id={axis: lax.rem(me + i, size)}, device_id_type=MESH,
            )
            for i in range(1, size)
        ]

    stat_moves = all_send(stat, "tp", t, n_tp, stat_send, stat_recv)
    for move in stat_moves:
        move.start()
    for move in stat_moves:
        move.wait_recv()
    sums = stat[0, 0:2, :]
    for i in range(1, n_tp):
        sums = sums + stat[i, 0:2, :]
    scale_row = lax.rsqrt(sums[0:1] / HID + EPSILON)
    factor_row = scale_row * scale_row * scale_row * sums[1:2] / HID
    scale = jnp.broadcast_to(scale_row, (HD, rows)).T
    factor = jnp.broadcast_to(factor_row, (HD, rows)).T

    def upstream(h):
        out = att[:, head(h)]
        grad = g_ref[:, head(h)].astype(F32)
        scaled = grad * scale
        up[:, head(h)] = (gain_ref[h:h + 1, :] * scaled - out * factor).astype(BF16)
        gain_seq[z, h:h + 1, :] = jnp.sum(scaled * out, axis=0, keepdims=True)

    def back_state(h):
        total_back[h] = dot(q_ref[:, head(h)], up[:, head(h)], 0, 0)
        if n_seq > 1:
            @pl.when(last)
            def _():
                for p in range(PIECES):
                    move_down(h, p).start()

    upstream(0)
    back_state(0)
    for h in range(1, heads):
        upstream(h)

    def gain_to_first(source):
        return pltpu.make_async_remote_copy(
            src_ref=gain_seq.at[source], dst_ref=gain_seq.at[source],
            send_sem=gs_send.at[source], recv_sem=gs_recv.at[source],
            device_id={"seq": 0}, device_id_type=MESH,
        )

    def gain_from_first(target):
        return pltpu.make_async_remote_copy(
            src_ref=gg, dst_ref=gain_back,
            send_sem=gb_send.at[target], recv_sem=gb_recv.at[target],
            device_id={"seq": target}, device_id_type=MESH,
        )

    @pl.when(jnp.logical_not(first))
    def _():
        gain_to_first(z).start()

    for h in range(1, heads):
        back_state(h)

    dp_moves = all_send(gain_dp, "dp", d, n_dp, gd_send, gd_recv)
    stores = []

    def store(src, dst):
        copy = pltpu.make_async_copy(src, dst, out_sem.at[len(stores)])
        copy.start()
        stores.append(copy)

    def normed_of(h):
        normed[:, head(h)] = (att[:, head(h)] * scale * gain_ref[h:h + 1, :]).astype(BF16)
        store(normed.at[:, head(h)], normed_out.at[:, head(h)])

    def mixed_of(h):
        mix = jnp.where(causal, dot(up[:, head(h)], v_ref[:, head(h)], 1, 1), 0.0)
        mixed[h] = mix.astype(BF16)

    def dq_of(h):
        dq[:, head(h)] = (
            dot(mixed[h], k_ref[:, head(h)], 1, 0) + dot_wide(up[:, head(h)], prior[h], 1, 1)
        ).astype(BF16)
        store(dq.at[:, head(h)], dq_out.at[:, head(h)])

    def block_parts(h):
        dk_part[h] = dot(mixed[h], q_ref[:, head(h)], 0, 0)
        dv_part[h] = dot(scores[h], up[:, head(h)], 0, 0)

    def dk_of(h):
        wide = dot_wide(v_ref[:, head(h)], later[h], 1, 1)
        dk[:, head(h)] = (dk_part[h] + wide).astype(BF16)
        store(dk.at[:, head(h)], dk_out.at[:, head(h)])

    def dv_of(h):
        wide = dot_wide(k_ref[:, head(h)], later[h], 1, 0)
        dv[:, head(h)] = (dv_part[h] + wide).astype(BF16)
        store(dv.at[:, head(h)], dv_out.at[:, head(h)])

    def gain_middle():
        @pl.when(first)
        def _():
            for source in range(1, n_seq):
                gain_to_first(source).wait_recv()
            gain_sum = gain_seq[0]
            for i in range(1, n_seq):
                gain_sum = gain_sum + gain_seq[i]
            gain_dp[d] = gain_sum
            for move in dp_moves:
                move.start()

    def gain_end():
        @pl.when(first)
        def _():
            for move in dp_moves:
                move.wait_recv()
            gain_sum = gain_dp[0]
            for i in range(1, n_dp):
                gain_sum = gain_sum + gain_dp[i]
            gg[...] = gain_sum
            for target in range(1, n_seq):
                gain_from_first(target).start()

    block_work = [
        functools.partial(work, h)
        for h in range(heads)
        for work in (mixed_of, dq_of, block_parts, normed_of)
    ]
    half = 2 * heads
    for step in block_work[:half]:
        step()
    slots = [[] for _ in range(heads * PIECES)]
    for h in range(heads):
        if h > 0:
            slots[h * PIECES].append(functools.partial(dk_of, h - 1))
            slots[h * PIECES + 1].append(functools.partial(dv_of, h - 1))
        slots[h * PIECES + 2].append(block_work[half + 2 * h])
        slots[h * PIECES + 3].append(block_work[half + 2 * h + 1])
    slots[0].append(gain_middle)
    slots[heads // 4 * PIECES].append(gain_end)
    relay_all(total_back, later, move_down, last, first, slots)
    dk_of(heads - 1)
    dv_of(heads - 1)

    gg_copy = pltpu.make_async_copy(gg, gg_out, out_sem.at[4 * heads])

    @pl.when(first)
    def _():
        gg_copy.start()
        for move in dp_moves:
            move.wait_send()
        for target in range(1, n_seq):
            gain_from_first(target).wait_send()

    back_copy = pltpu.make_async_copy(gain_back, gg_out, out_sem.at[4 * heads])

    @pl.when(jnp.logical_not(first))
    def _():
        gain_from_first(z).wait_recv()
        back_copy.start()
        gain_to_first(z).wait_send()

    for move in stat_moves:
        move.wait_send()
    if n_seq > 1:
        @pl.when(jnp.logical_not(last))
        def _():
            for h in range(heads):
                for p in range(PIECES):
                    move_up(h, p).wait_send()

        @pl.when(jnp.logical_not(first))
        def _():
            for h in range(heads):
                for p in range(PIECES):
                    move_down(h, p).wait_send()
    for copy in stores:
        copy.wait()

    @pl.when(first)
    def _():
        gg_copy.wait()

    @pl.when(jnp.logical_not(first))
    def _():
        back_copy.wait()


def helped(
    n_tp, n_dp,
    q_in, k_in, v_in, gain_in, g_in,
    normed_out, dq_out, dk_out, dv_out, gg_out,
    q_ref, k_ref, v_ref, gain_ref, g_ref,
    prior, total, later, total_back,
    att, scores, mixed, squares, crossed, dk_part, dv_part, up, normed, dq, dk, dv,
    early_out, early_in, help_att,
    stat, gain_seq, gain_dp, gg, gain_back,
    in_sem, out_sem,
    up_send, up_recv, down_send, down_recv,
    early_send, early_recv,
    stat_send, stat_recv, gs_send, gs_recv, gd_send, gd_recv,
    gb_send, gb_recv,
):
    rows, width = q_ref.shape
    heads = width // HD
    far, near = heads - 1, (heads - 2, heads - 3)
    common = tuple(range(heads - 3))
    order_down = (far,) + near + common
    z = lax.axis_index("seq")
    t = lax.axis_index("tp")
    d = lax.axis_index("dp")
    slot = z * n_tp + t

    def head(h):
        return slice(h * HD, (h + 1) * HD)

    def part(p):
        return slice(p * PART, (p + 1) * PART)

    def tp_peer(i):
        return lax.rem(t + i, n_tp)

    causal = lax.broadcasted_iota(jnp.int32, (rows, rows), 0) >= lax.broadcasted_iota(
        jnp.int32, (rows, rows), 1
    )
    loads = [
        pltpu.make_async_copy(src, dst, in_sem.at[i])
        for i, (src, dst) in enumerate(
            [(k_in, k_ref), (v_in, v_ref), (q_in, q_ref), (g_in, g_ref), (gain_in, gain_ref)]
        )
    ]

    def program(own):
        barrier = pltpu.get_barrier_semaphore()
        greeted = [{"tp": tp_peer(i)} for i in range(1, n_tp)]
        heard = len(greeted)
        if own == 0:
            greeted += [{"dp": lax.rem(d + i, n_dp)} for i in range(1, n_dp)]
            heard = len(greeted) + 1
        else:
            heard += 2
        greeted += [{"seq": i} for i in ((1,), (0, 2, 3), (1, 3), (2,))[own]]
        for peer in greeted:
            pl.semaphore_signal(barrier, inc=1, device_id=peer, device_id_type=MESH)
        for load in loads:
            load.start()

        stores, sent = [], []

        def send(move):
            move.start()
            sent.append(move)

        def store(src, dst):
            copy = pltpu.make_async_copy(src, dst, out_sem.at[len(stores)])
            copy.start()
            stores.append(copy)

        def move_up(h, p):
            i = h * PIECES + p
            return pltpu.make_async_remote_copy(
                src_ref=total.at[h, part(p)], dst_ref=prior.at[h, part(p)],
                send_sem=up_send.at[i], recv_sem=up_recv.at[i],
                device_id={"seq": min(own + 1, 3)}, device_id_type=MESH,
            )

        def move_down(h, p):
            i = h * PIECES + p
            return pltpu.make_async_remote_copy(
                src_ref=total_back.at[h, part(p)], dst_ref=later.at[h, part(p)],
                send_sem=down_send.at[i], recv_sem=down_recv.at[i],
                device_id={"seq": max(own - 1, 0)}, device_id_type=MESH,
            )

        def arrive(move, h):
            for p in range(PIECES):
                move(h, p).wait_recv()

        def move_early(i, j, target):
            return pltpu.make_async_remote_copy(
                src_ref=early_out.at[i], dst_ref=early_in.at[j],
                send_sem=early_send.at[i], recv_sem=early_recv.at[j],
                device_id={"seq": target}, device_id_type=MESH,
            )

        def early_arrive(j, source):
            move_early(0, j, source).wait_recv()

        def total_of(h):
            total[h] = dot(k_ref[:, head(h)], v_ref[:, head(h)], 0, 0)

        def score_of(h):
            score = jnp.where(causal, dot(q_ref[:, head(h)], k_ref[:, head(h)], 1, 1), 0.0)
            scores[h] = score.astype(BF16)

        def attend_block(h):
            att[:, head(h)] = dot(scores[h], v_ref[:, head(h)], 1, 0)

        def attend_prior(h):
            att[:, head(h)] = att[:, head(h)] + dot_wide(q_ref[:, head(h)], prior[h], 1, 0)

        counted = set()

        def count(i, out, weighted):
            square, cross = out * out, weighted * out
            squares[i] = squares[i] + square if i in counted else square
            crossed[i] = crossed[i] + cross if i in counted else cross
            counted.add(i)

        def add_stats(h):
            count(0, att[:, head(h)], g_ref[:, head(h)].astype(F32) * gain_ref[h:h + 1, :])

        def send_early(h, first, slots, target, state=None):
            early_out[first] = q_ref[:, head(h)].astype(F32)
            send(move_early(first, slots, target))
            early_out[first + 1] = g_ref[:, head(h)].astype(F32)
            send(move_early(first + 1, slots + 1, target))
            score_of(h)
            local = dot(scores[h], v_ref[:, head(h)], 1, 0)
            att[:, head(h)] = local
            if state is not None:
                early_arrive(state, 2)
                local = local + dot_wide(q_ref[:, head(h)], early_in[state], 1, 0)
            early_out[first + 2] = local
            send(move_early(first + 2, slots + 2, target))

        def help_attend(j, first, h, state, i):
            for n in range(first, first + 3):
                early_arrive(n, own + max(i, 1))
            out = early_in[first + 2] + dot_wide(early_in[first].astype(BF16), state, 1, 0)
            help_att[j] = out
            if i:
                count(i, out, early_in[first + 1] * gain_ref[h:h + 1, :])

        def help_back(j, first, h, factors):
            scaled = early_in[first + 1] * factors[0]
            grad = (gain_ref[h:h + 1, :] * scaled - help_att[j] * factors[1]).astype(BF16)
            return dot(early_in[first].astype(BF16), grad, 0, 0)

        def relay(mine, come, move, order, slots, start=True):
            slots = list(slots)
            for h in order:
                for p in range(PIECES):
                    move(h, p).wait_recv()
                    mine[h, part(p)] = mine[h, part(p)] + come[h, part(p)]
                    send(move(h, p))
                    if slots:
                        slots.pop(0)()
            for step in slots:
                step()

        def put_stats():
            for i in sorted(counted):
                b = 2 * (own + i)
                stat[slot, b:b + 1, :] = jnp.sum(squares[i].T, axis=0, keepdims=True)
                stat[slot, b + 1:b + 2, :] = jnp.sum(crossed[i].T, axis=0, keepdims=True)

        def stat_move(n, target, i):
            return pltpu.make_async_remote_copy(
                src_ref=stat.at[slot], dst_ref=stat.at[slot],
                send_sem=stat_send.at[n], recv_sem=stat_recv.at[slot],
                device_id={"seq": target, "tp": tp_peer(i)}, device_id_type=MESH,
            )

        def send_stats():
            n = 0
            for target in ((0,), (1, 3, 2), (2, 3, 1), (3, 2, 1))[own]:
                for i in range(1 if target == own else 0, n_tp):
                    send(stat_move(n, target, i))
                    n += 1

        def sum_stats(source):
            for i in range(1 if source == own else 0, n_tp):
                s = source * n_tp + tp_peer(i)
                pltpu.make_async_remote_copy(
                    src_ref=stat.at[s], dst_ref=stat.at[s],
                    send_sem=stat_send.at[0], recv_sem=stat_recv.at[s],
                    device_id={"tp": tp_peer(1)}, device_id_type=MESH,
                ).wait_recv()
            total_stat = stat[source * n_tp]
            for i in range(1, n_tp):
                total_stat = total_stat + stat[source * n_tp + i]
            return total_stat

        def factors_of(sums, b):
            scale = lax.rsqrt(sums[2 * b:2 * b + 1] / HID + EPSILON)
            factor = scale * scale * scale * sums[2 * b + 1:2 * b + 2] / HID
            return tuple(jnp.broadcast_to(x, (HD, rows)).T for x in (scale, factor))

        def upstream(h, factors):
            out = att[:, head(h)]
            scaled = g_ref[:, head(h)].astype(F32) * factors[0]
            up[:, head(h)] = (gain_ref[h:h + 1, :] * scaled - out * factors[1]).astype(BF16)
            gain_seq[own, h:h + 1, :] = jnp.sum(scaled * out, axis=0, keepdims=True)

        def back_state(h):
            total_back[h] = dot(q_ref[:, head(h)], up[:, head(h)], 0, 0)

        def send_down(h):
            for p in range(PIECES):
                send(move_down(h, p))

        def gain_to_first(source):
            return pltpu.make_async_remote_copy(
                src_ref=gain_seq.at[source], dst_ref=gain_seq.at[source],
                send_sem=gs_send.at[source], recv_sem=gs_recv.at[source],
                device_id={"seq": 0}, device_id_type=MESH,
            )

        def gain_from_first(target):
            return pltpu.make_async_remote_copy(
                src_ref=gg, dst_ref=gain_back,
                send_sem=gb_send.at[target], recv_sem=gb_recv.at[target],
                device_id={"seq": target}, device_id_type=MESH,
            )

        def normed_of(h, factors):
            normed[:, head(h)] = (
                att[:, head(h)] * factors[0] * gain_ref[h:h + 1, :]
            ).astype(BF16)
            store(normed.at[:, head(h)], normed_out.at[:, head(h)])

        def mixed_of(h):
            mix = jnp.where(causal, dot(up[:, head(h)], v_ref[:, head(h)], 1, 1), 0.0)
            mixed[h] = mix.astype(BF16)

        def dq_of(h):
            wide = dot(mixed[h], k_ref[:, head(h)], 1, 0)
            if own > 0:
                wide = wide + dot_wide(up[:, head(h)], prior[h], 1, 1)
            dq[:, head(h)] = wide.astype(BF16)
            store(dq.at[:, head(h)], dq_out.at[:, head(h)])

        def block_parts(h):
            dk_part[h] = dot(mixed[h], q_ref[:, head(h)], 0, 0)
            dv_part[h] = dot(scores[h], up[:, head(h)], 0, 0)

        def dk_of(h):
            wide = dk_part[h]
            if own < 3:
                wide = wide + dot_wide(v_ref[:, head(h)], later[h], 1, 1)
            dk[:, head(h)] = wide.astype(BF16)
            store(dk.at[:, head(h)], dk_out.at[:, head(h)])

        def dv_of(h):
            wide = dv_part[h]
            if own < 3:
                wide = wide + dot_wide(k_ref[:, head(h)], later[h], 1, 0)
            dv[:, head(h)] = wide.astype(BF16)
            store(dv.at[:, head(h)], dv_out.at[:, head(h)])

        def local_work(h, factors):
            return [
                functools.partial(mixed_of, h),
                functools.partial(dq_of, h),
                functools.partial(block_parts, h),
                functools.partial(normed_of, h, factors),
            ]

        def last_work(h):
            return [functools.partial(dk_of, h), functools.partial(dv_of, h)]

        def run(steps):
            for step in steps:
                step()

        def forward_slots(order, extra):
            slots, held = [], []
            for h in order:
                slots += [functools.partial(score_of, h), functools.partial(attend_block, h)]
                slots += held if held else [lambda: None] * 2
                held = extra(h)
            return slots + held

        stat[slot] = jnp.zeros_like(stat[slot])
        for load in loads:
            load.wait()

        if own == 0:
            for h in range(heads):
                total_of(h)
                if h == 0:
                    pl.semaphore_wait(barrier, heard)
                for p in range(PIECES):
                    send(move_up(h, p))
            for h in range(heads):
                score_of(h)
                attend_block(h)
                add_stats(h)
            put_stats()
            send_stats()
            factors = factors_of(sum_stats(0), 0)
            for h in range(heads):
                upstream(h, factors)
            for h in range(heads):
                run(local_work(h, factors))
            gains = [{"dp": lax.rem(d + i, n_dp)} for i in range(1, n_dp)]
            gain_moves = [
                pltpu.make_async_remote_copy(
                    src_ref=gain_dp.at[d], dst_ref=gain_dp.at[d],
                    send_sem=gd_send.at[i], recv_sem=gd_recv.at[i],
                    device_id=peer, device_id_type=MESH,
                )
                for i, peer in enumerate(gains)
            ]
            for n, h in enumerate(order_down):
                arrive(move_down, h)
                run(last_work(h))
                if n == 0:
                    for source in range(1, 4):
                        gain_to_first(source).wait_recv()
                    gain_dp[d] = (gain_seq[0] + gain_seq[1]) + (gain_seq[2] + gain_seq[3])
                    for move in gain_moves:
                        send(move)
                if n == 2:
                    for move in gain_moves:
                        move.wait_recv()
                    gain_sum = gain_dp[0]
                    for i in range(1, n_dp):
                        gain_sum = gain_sum + gain_dp[i]
                    gg[...] = gain_sum
                    for target in range(1, 4):
                        send(gain_from_first(target))
                    store(gg, gg_out)

        if own == 1:
            pl.semaphore_wait(barrier, heard)
            for h in range(heads):
                total_of(h)
            relay(total, prior, move_up, range(heads), forward_slots(
                range(heads),
                lambda h: [functools.partial(attend_prior, h), functools.partial(add_stats, h)],
            ))
            help_attend(0, 3, far, total[far], 1)
            help_attend(1, 0, far, total[far], 2)
            put_stats()
            send_stats()
            sums = sum_stats(1)
            factors = factors_of(sums, 1)
            for h in order_down:
                upstream(h, factors)
                back_state(h)
            send(gain_to_first(own))
            sums = sums + sum_stats(2)
            beyond = help_back(0, 3, far, factors_of(sums, 2))
            total_back[far] = total_back[far] + beyond
            sums = sums + sum_stats(3)
            last = help_back(1, 0, far, factors_of(sums, 3))
            total_back[far] = total_back[far] + last
            send_down(far)
            later[far] = beyond + last
            steps = local_work(far, factors) + last_work(far)
            for h in near + common:
                steps += local_work(h, factors)
            run(steps[:10])
            relay(total_back, later, move_down, near + common, steps[10:])
            for h in near + common:
                run(last_work(h))

        if own == 2:
            total_of(far)
            early_out[3] = total[far]
            pl.semaphore_wait(barrier, heard)
            send(move_early(3, 0, 3))
            send_early(far, 0, 3, 1)
            for h in range(heads - 1):
                total_of(h)
            score_of(near[0])
            attend_block(near[0])

            def own_part(h):
                return [functools.partial(attend_prior, h), functools.partial(add_stats, h)]

            slots = forward_slots(range(heads - 2), own_part)
            relay(total, prior, move_up, range(heads - 1), slots)
            run(own_part(near[0]))
            help_attend(0, 0, near[0], total[near[0]], 1)
            help_attend(1, 3, near[1], total[near[1]], 1)
            put_stats()
            send_stats()
            relay(total, prior, move_up, (far,), ())
            attend_prior(far)
            sums = sum_stats(1) + sum_stats(2)
            factors = factors_of(sums, 2)
            for h in near:
                upstream(h, factors)
                back_state(h)
            sums = sums + sum_stats(3)
            ahead = factors_of(sums, 3)
            for j, h in enumerate(near):
                beyond = help_back(j, 3 * j, h, ahead)
                total_back[h] = total_back[h] + beyond
                send_down(h)
                later[h] = beyond
            for h in common:
                upstream(h, factors)
                back_state(h)
            upstream(far, factors)
            send(gain_to_first(own))
            steps = []
            for h in near:
                steps += local_work(h, factors) + last_work(h)
            for h in common + (far,):
                steps += local_work(h, factors)
            relay(total_back, later, move_down, common, steps)
            for h in common:
                run(last_work(h))
            arrive(move_down, far)
            run(last_work(far))

        if own == 3:
            pl.semaphore_wait(barrier, heard)
            send_early(near[0], 3, 0, 2)
            send_early(far, 0, 0, 1, 0)
            send_early(near[1], 6, 3, 2)
            for h in common:
                score_of(h)
                attend_block(h)
            for h in common:
                arrive(move_up, h)
                attend_prior(h)
                add_stats(h)
            put_stats()
            send_stats()
            arrive(move_up, near[1])
            attend_prior(near[1])
            sums = sum_stats(1) + sum_stats(2)
            sums = sums + sum_stats(3)
            factors = factors_of(sums, 3)
            for h in common:
                upstream(h, factors)
                back_state(h)
                send_down(h)
            for h in (near[0], far):
                arrive(move_up, h)
                attend_prior(h)
            for h in near + (far,):
                upstream(h, factors)
            send(gain_to_first(own))
            back_state(far)
            send_down(far)
            for h in range(heads):
                run(local_work(h, factors))
                run(last_work(h))

        if own > 0:
            gain_from_first(own).wait_recv()
            store(gain_back, gg_out)
        for move in sent:
            move.wait_send()
        for copy in stores:
            copy.wait()

    for own in range(4):
        pl.when(z == own)(functools.partial(program, own))


def write_out(*refs):
    copies = [pltpu.make_async_copy(refs[i], refs[5 + i], refs[10].at[i]) for i in range(5)]
    for copy in copies:
        copy.start()
    for copy in copies:
        copy.wait()


def solution(mesh):
    n_seq, n_tp, n_dp = (mesh.shape[name] for name in ("seq", "tp", "dp"))

    def local(queries, keys, values, out_gain, grad_out):
        shape = queries.shape
        rows, width = shape[0] * shape[1], shape[2]
        heads = width // HD
        chunks = heads * PIECES
        matrix = jax.ShapeDtypeStruct((rows, width), BF16)
        state = pltpu.VMEM((heads, HD, HD), F32)
        page = pltpu.VMEM((rows, width), BF16)
        tile = lambda *lead: pltpu.VMEM((*lead, rows, HD), F32)
        sems = pltpu.SemaphoreType.DMA
        flat = lambda x: x.reshape(rows, width)
        with_help = n_seq == 4 and rows == HD and heads >= 4
        if with_help:
            body = functools.partial(helped, n_tp, n_dp)
            sums, stats = tile(3), n_seq * n_tp
            early = [tile(9), tile(6), tile(2)]
            early_sems = [sems((9,)), sems((6,))]
            stat_sems = [sems((3 * n_tp,)), sems((n_seq * n_tp,))]
        else:
            body = functools.partial(kernel, n_seq, n_tp, n_dp)
            sums, stats, early, early_sems = tile(), n_tp, [], []
            stat_sems = [sems((max(n_tp - 1, 1),)), sems((max(n_tp - 1, 1),))]
        outs = pl.pallas_call(
            body,
            out_shape=(matrix,) * 4 + (jax.ShapeDtypeStruct((heads, HD), F32),),
            in_specs=[pl.BlockSpec(memory_space=pltpu.HBM)] * 5,
            out_specs=[pl.BlockSpec(memory_space=pl.ANY)] * 5,
            scratch_shapes=[
                page, page, page, pltpu.VMEM((heads, HD), F32), page,
                state, state, state, state,
                pltpu.VMEM((rows, width), F32),
                pltpu.VMEM((heads, rows, rows), BF16), pltpu.VMEM((heads, rows, rows), BF16),
                sums, sums, tile(heads), tile(heads),
                page, page, page, page, page,
                *early,
                pltpu.VMEM((stats, 8, rows), F32),
                pltpu.VMEM((n_seq, heads, HD), F32),
                pltpu.VMEM((n_dp, heads, HD), F32),
                pltpu.VMEM((heads, HD), F32), pltpu.VMEM((heads, HD), F32),
                sems((5,)), sems((4 * heads + 1,)),
                sems((chunks,)), sems((chunks,)), sems((chunks,)), sems((chunks,)),
                *early_sems,
                *stat_sems,
                sems((n_seq,)), sems((n_seq,)),
                sems((max(n_dp - 1, 1),)), sems((max(n_dp - 1, 1),)),
                sems((n_seq,)), sems((n_seq,)),
            ],
            compiler_params=pltpu.CompilerParams(
                collective_id=0, has_side_effects=True, vmem_limit_bytes=32 << 20
            ),
        )(
            *(
                pltpu.with_memory_space_constraint(x, pltpu.HBM)
                for x in (
                    flat(queries), flat(keys), flat(values),
                    out_gain.reshape(heads, HD), flat(grad_out),
                )
            )
        )
        outs = pl.pallas_call(
            write_out,
            out_shape=tuple(jax.ShapeDtypeStruct(x.shape, x.dtype) for x in outs),
            in_specs=[pl.BlockSpec(memory_space=pl.ANY)] * 5,
            out_specs=[pl.BlockSpec(memory_space=pl.ANY)] * 5,
            scratch_shapes=[sems((5,))],
            compiler_params=pltpu.CompilerParams(vmem_limit_bytes=8 << 20),
        )(*outs)
        return tuple(x.reshape(shape) for x in outs[:4]) + (outs[4].reshape(width),)

    spec = P("dp", "seq", "tp")
    return jax.shard_map(
        local,
        mesh=mesh,
        in_specs=(spec, spec, spec, P("tp"), spec),
        out_specs=(spec, spec, spec, spec, P("tp")),
        check_vma=False,
    )
```

```python
import functools

import jax
import jax.numpy as jnp
from jax import lax
from jax.experimental import pallas as pl
from jax.experimental.pallas import tpu as pltpu
from jax.sharding import PartitionSpec as P

HD = 128
HID = 4096
EPSILON = 1e-06
PIECES = 4
PART = HD // PIECES
MESH = pl.DeviceIdType.MESH
F32 = jnp.float32
BF16 = jnp.bfloat16


def dot(a, b, ca, cb):
    return lax.dot_general(a, b, (((ca,), (cb,)), ((), ())), preferred_element_type=F32)


def split(x):
    high = x.astype(BF16)
    return high, (x - high.astype(F32)).astype(BF16)


def dot_wide(a, x, ca, cb):
    high, low = split(x)
    return dot(a, high, ca, cb) + dot(a, low, ca, cb)


def kernel(
    n_seq, n_tp, n_dp,
    q_in, k_in, v_in, gain_in, g_in,
    normed_out, dq_out, dk_out, dv_out, gg_out,
    q_ref, k_ref, v_ref, gain_ref, g_ref,
    prior, total, later, total_back,
    att, scores, mixed, squares, crossed, dk_part, dv_part, up, normed, dq, dk, dv,
    stat, gain_seq, gain_dp, gg, gain_back,
    in_sem, out_sem,
    up_send, up_recv, down_send, down_recv,
    stat_send, stat_recv, gs_send, gs_recv, gd_send, gd_recv,
    gb_send, gb_recv,
):
    rows, width = q_ref.shape
    heads = width // HD
    z = lax.axis_index("seq")
    t = lax.axis_index("tp")
    d = lax.axis_index("dp")
    first, last = z == 0, z == n_seq - 1
    above = lax.rem(z + 1, n_seq)
    below = lax.rem(z + n_seq - 1, n_seq)

    def head(h):
        return slice(h * HD, (h + 1) * HD)

    def peers(axis, me, size):
        return [{axis: lax.rem(me + i, size)} for i in range(1, size)]

    greeted = peers("tp", t, n_tp) + peers("dp", d, n_dp)
    if n_seq > 1:
        greeted.append({"seq": below})
    barrier = pltpu.get_barrier_semaphore()
    for peer in greeted:
        pl.semaphore_signal(barrier, inc=1, device_id=peer, device_id_type=MESH)

    loads = [
        pltpu.make_async_copy(src, dst, in_sem.at[i])
        for i, (src, dst) in enumerate(
            [(k_in, k_ref), (v_in, v_ref), (q_in, q_ref), (g_in, g_ref), (gain_in, gain_ref)]
        )
    ]
    for load in loads:
        load.start()
    loads[0].wait()
    loads[1].wait()

    def part(p):
        return slice(p * PART, (p + 1) * PART)

    def move_up(h, p):
        i = h * PIECES + p
        return pltpu.make_async_remote_copy(
            src_ref=total.at[h, part(p)], dst_ref=prior.at[h, part(p)],
            send_sem=up_send.at[i], recv_sem=up_recv.at[i],
            device_id={"seq": above}, device_id_type=MESH,
        )

    def move_down(h, p):
        i = h * PIECES + p
        return pltpu.make_async_remote_copy(
            src_ref=total_back.at[h, part(p)], dst_ref=later.at[h, part(p)],
            send_sem=down_send.at[i], recv_sem=down_recv.at[i],
            device_id={"seq": below}, device_id_type=MESH,
        )

    def relay(h, p, mine, come, move, is_first, is_last):
        @pl.when(jnp.logical_and(jnp.logical_not(is_first), jnp.logical_not(is_last)))
        def _():
            move(h, p).wait_recv()
            mine[h, part(p)] = mine[h, part(p)] + come[h, part(p)]
            move(h, p).start()

        @pl.when(jnp.logical_and(is_last, jnp.logical_not(is_first)))
        def _():
            move(h, p).wait_recv()

    def relay_all(mine, come, move, is_first, is_last, slots):
        for h in range(heads):
            for p in range(PIECES):
                relay(h, p, mine, come, move, is_first, is_last)
                for step in slots[h * PIECES + p]:
                    step()

    for h in range(heads):
        total[h] = dot(k_ref[:, head(h)], v_ref[:, head(h)], 0, 0)
        if h == 0:
            pl.semaphore_wait(barrier, len(greeted))
        if n_seq > 1:
            @pl.when(first)
            def _():
                for p in range(PIECES):
                    move_up(h, p).start()

    @pl.when(first)
    def _():
        prior[...] = jnp.zeros_like(prior)

    @pl.when(last)
    def _():
        later[...] = jnp.zeros_like(later)

    loads[2].wait()
    loads[3].wait()
    loads[4].wait()
    causal = lax.broadcasted_iota(jnp.int32, (rows, rows), 0) >= lax.broadcasted_iota(
        jnp.int32, (rows, rows), 1
    )
    def score_of(h):
        score = jnp.where(causal, dot(q_ref[:, head(h)], k_ref[:, head(h)], 1, 1), 0.0)
        scores[h] = score.astype(BF16)

    def attend_block(h):
        att[:, head(h)] = dot(scores[h], v_ref[:, head(h)], 1, 0)

    def attend_prior(h):
        att[:, head(h)] = att[:, head(h)] + dot_wide(q_ref[:, head(h)], prior[h], 1, 0)

    def add_stats(h):
        out = att[:, head(h)]
        square = out * out
        cross = g_ref[:, head(h)].astype(F32) * gain_ref[h:h + 1, :] * out
        squares[...] = square if h == 0 else squares[...] + square
        crossed[...] = cross if h == 0 else crossed[...] + cross

    slots = [[] for _ in range(heads * PIECES)]
    for h in range(heads):
        slots[h * PIECES].append(functools.partial(score_of, h))
        slots[h * PIECES + 1].append(functools.partial(attend_block, h))
        if h > 0:
            slots[h * PIECES + 2].append(functools.partial(attend_prior, h - 1))
            slots[h * PIECES + 3].append(functools.partial(add_stats, h - 1))
    relay_all(total, prior, move_up, first, last, slots)
    attend_prior(heads - 1)
    add_stats(heads - 1)

    stat[t, 0:1, :] = jnp.sum(squares[...].T, axis=0, keepdims=True)
    stat[t, 1:2, :] = jnp.sum(crossed[...].T, axis=0, keepdims=True)

    def all_send(buffer, axis, me, size, send, recv):
        return [
            pltpu.make_async_remote_copy(
                src_ref=buffer.at[me], dst_ref=buffer.at[me],
                send_sem=send.at[i - 1], recv_sem=recv.at[i - 1],
                device_id={axis: lax.rem(me + i, size)}, device_id_type=MESH,
            )
            for i in range(1, size)
        ]

    stat_moves = all_send(stat, "tp", t, n_tp, stat_send, stat_recv)
    for move in stat_moves:
        move.start()
    for move in stat_moves:
        move.wait_recv()
    sums = stat[0, 0:2, :]
    for i in range(1, n_tp):
        sums = sums + stat[i, 0:2, :]
    scale_row = lax.rsqrt(sums[0:1] / HID + EPSILON)
    factor_row = scale_row * scale_row * scale_row * sums[1:2] / HID
    scale = jnp.broadcast_to(scale_row, (HD, rows)).T
    factor = jnp.broadcast_to(factor_row, (HD, rows)).T

    def upstream(h):
        out = att[:, head(h)]
        grad = g_ref[:, head(h)].astype(F32)
        scaled = grad * scale
        up[:, head(h)] = (gain_ref[h:h + 1, :] * scaled - out * factor).astype(BF16)
        gain_seq[z, h:h + 1, :] = jnp.sum(scaled * out, axis=0, keepdims=True)

    def back_state(h):
        total_back[h] = dot(q_ref[:, head(h)], up[:, head(h)], 0, 0)
        if n_seq > 1:
            @pl.when(last)
            def _():
                for p in range(PIECES):
                    move_down(h, p).start()

    upstream(0)
    back_state(0)
    for h in range(1, heads):
        upstream(h)

    def gain_to_first(source):
        return pltpu.make_async_remote_copy(
            src_ref=gain_seq.at[source], dst_ref=gain_seq.at[source],
            send_sem=gs_send.at[source], recv_sem=gs_recv.at[source],
            device_id={"seq": 0}, device_id_type=MESH,
        )

    def gain_from_first(target):
        return pltpu.make_async_remote_copy(
            src_ref=gg, dst_ref=gain_back,
            send_sem=gb_send.at[target], recv_sem=gb_recv.at[target],
            device_id={"seq": target}, device_id_type=MESH,
        )

    @pl.when(jnp.logical_not(first))
    def _():
        gain_to_first(z).start()

    for h in range(1, heads):
        back_state(h)

    dp_moves = all_send(gain_dp, "dp", d, n_dp, gd_send, gd_recv)
    stores = []

    def store(src, dst):
        copy = pltpu.make_async_copy(src, dst, out_sem.at[len(stores)])
        copy.start()
        stores.append(copy)

    def normed_of(h):
        normed[:, head(h)] = (att[:, head(h)] * scale * gain_ref[h:h + 1, :]).astype(BF16)
        store(normed.at[:, head(h)], normed_out.at[:, head(h)])

    def mixed_of(h):
        mix = jnp.where(causal, dot(up[:, head(h)], v_ref[:, head(h)], 1, 1), 0.0)
        mixed[h] = mix.astype(BF16)

    def dq_of(h):
        dq[:, head(h)] = (
            dot(mixed[h], k_ref[:, head(h)], 1, 0) + dot_wide(up[:, head(h)], prior[h], 1, 1)
        ).astype(BF16)
        store(dq.at[:, head(h)], dq_out.at[:, head(h)])

    def block_parts(h):
        dk_part[h] = dot(mixed[h], q_ref[:, head(h)], 0, 0)
        dv_part[h] = dot(scores[h], up[:, head(h)], 0, 0)

    def dk_of(h):
        wide = dot_wide(v_ref[:, head(h)], later[h], 1, 1)
        dk[:, head(h)] = (dk_part[h] + wide).astype(BF16)
        store(dk.at[:, head(h)], dk_out.at[:, head(h)])

    def dv_of(h):
        wide = dot_wide(k_ref[:, head(h)], later[h], 1, 0)
        dv[:, head(h)] = (dv_part[h] + wide).astype(BF16)
        store(dv.at[:, head(h)], dv_out.at[:, head(h)])

    def gain_middle():
        @pl.when(first)
        def _():
            for source in range(1, n_seq):
                gain_to_first(source).wait_recv()
            gain_sum = gain_seq[0]
            for i in range(1, n_seq):
                gain_sum = gain_sum + gain_seq[i]
            gain_dp[d] = gain_sum
            for move in dp_moves:
                move.start()

    def gain_end():
        @pl.when(first)
        def _():
            for move in dp_moves:
                move.wait_recv()
            gain_sum = gain_dp[0]
            for i in range(1, n_dp):
                gain_sum = gain_sum + gain_dp[i]
            gg[...] = gain_sum
            for target in range(1, n_seq):
                gain_from_first(target).start()

    block_work = [
        functools.partial(work, h)
        for h in range(heads)
        for work in (mixed_of, dq_of, block_parts, normed_of)
    ]
    half = 2 * heads
    for step in block_work[:half]:
        step()
    slots = [[] for _ in range(heads * PIECES)]
    for h in range(heads):
        if h > 0:
            slots[h * PIECES].append(functools.partial(dk_of, h - 1))
            slots[h * PIECES + 1].append(functools.partial(dv_of, h - 1))
        slots[h * PIECES + 2].append(block_work[half + 2 * h])
        slots[h * PIECES + 3].append(block_work[half + 2 * h + 1])
    slots[0].append(gain_middle)
    slots[heads // 4 * PIECES].append(gain_end)
    relay_all(total_back, later, move_down, last, first, slots)
    dk_of(heads - 1)
    dv_of(heads - 1)

    gg_copy = pltpu.make_async_copy(gg, gg_out, out_sem.at[4 * heads])

    @pl.when(first)
    def _():
        gg_copy.start()
        for move in dp_moves:
            move.wait_send()
        for target in range(1, n_seq):
            gain_from_first(target).wait_send()

    back_copy = pltpu.make_async_copy(gain_back, gg_out, out_sem.at[4 * heads])

    @pl.when(jnp.logical_not(first))
    def _():
        gain_from_first(z).wait_recv()
        back_copy.start()
        gain_to_first(z).wait_send()

    for move in stat_moves:
        move.wait_send()
    if n_seq > 1:
        @pl.when(jnp.logical_not(last))
        def _():
            for h in range(heads):
                for p in range(PIECES):
                    move_up(h, p).wait_send()

        @pl.when(jnp.logical_not(first))
        def _():
            for h in range(heads):
                for p in range(PIECES):
                    move_down(h, p).wait_send()
    for copy in stores:
        copy.wait()

    @pl.when(first)
    def _():
        gg_copy.wait()

    @pl.when(jnp.logical_not(first))
    def _():
        back_copy.wait()


def helped(
    n_tp, n_dp,
    q_in, k_in, v_in, gain_in, g_in,
    normed_out, dq_out, dk_out, dv_out, gg_out,
    q_ref, k_ref, v_ref, gain_ref, g_ref,
    prior, total, later, total_back,
    att, scores, mixed, squares, crossed, dk_part, dv_part, up,
    early_out, early_in, help_att,
    stat, gain_seq, gain_dp, gg, gain_back,
    in_sem,
    up_send, up_recv, down_send, down_recv,
    early_send, early_recv,
    stat_send, stat_recv, gs_send, gs_recv, gd_send, gd_recv,
    gb_send, gb_recv,
):
    rows, width = q_ref.shape
    heads = width // HD
    far, near = heads - 1, (heads - 2, heads - 3)
    common = tuple(range(heads - 3))
    order_down = (far,) + near + common
    z = lax.axis_index("seq")
    t = lax.axis_index("tp")
    d = lax.axis_index("dp")
    slot = z * n_tp + t

    def head(h):
        return slice(h * HD, (h + 1) * HD)

    def part(p):
        return slice(p * PART, (p + 1) * PART)

    def tp_peer(i):
        return lax.rem(t + i, n_tp)

    causal = lax.broadcasted_iota(jnp.int32, (rows, rows), 0) >= lax.broadcasted_iota(
        jnp.int32, (rows, rows), 1
    )
    loads = [
        pltpu.make_async_copy(src, dst, in_sem.at[i])
        for i, (src, dst) in enumerate(
            [(k_in, k_ref), (v_in, v_ref), (q_in, q_ref), (g_in, g_ref), (gain_in, gain_ref)]
        )
    ]

    def program(own):
        barrier = pltpu.get_barrier_semaphore()
        greeted = [{"tp": tp_peer(i)} for i in range(1, n_tp)]
        heard = len(greeted)
        if own == 0:
            greeted += [{"dp": lax.rem(d + i, n_dp)} for i in range(1, n_dp)]
            heard = len(greeted) + 1
        else:
            heard += 2
        greeted += [{"seq": i} for i in ((1,), (0, 2, 3), (1, 3), (2,))[own]]
        for peer in greeted:
            pl.semaphore_signal(barrier, inc=1, device_id=peer, device_id_type=MESH)
        for load in loads:
            load.start()

        sent = []

        def send(move):
            move.start()
            sent.append(move)

        def move_up(h, p):
            i = h * PIECES + p
            return pltpu.make_async_remote_copy(
                src_ref=total.at[h, part(p)], dst_ref=prior.at[h, part(p)],
                send_sem=up_send.at[i], recv_sem=up_recv.at[i],
                device_id={"seq": min(own + 1, 3)}, device_id_type=MESH,
            )

        def move_down(h, p):
            i = h * PIECES + p
            return pltpu.make_async_remote_copy(
                src_ref=total_back.at[h, part(p)], dst_ref=later.at[h, part(p)],
                send_sem=down_send.at[i], recv_sem=down_recv.at[i],
                device_id={"seq": max(own - 1, 0)}, device_id_type=MESH,
            )

        def arrive(move, h):
            for p in range(PIECES):
                move(h, p).wait_recv()

        def move_early(i, j, target):
            return pltpu.make_async_remote_copy(
                src_ref=early_out.at[i], dst_ref=early_in.at[j],
                send_sem=early_send.at[i], recv_sem=early_recv.at[j],
                device_id={"seq": target}, device_id_type=MESH,
            )

        def early_arrive(j, source):
            move_early(0, j, source).wait_recv()

        def total_of(h):
            total[h] = dot(k_ref[:, head(h)], v_ref[:, head(h)], 0, 0)

        def score_of(h):
            score = jnp.where(causal, dot(q_ref[:, head(h)], k_ref[:, head(h)], 1, 1), 0.0)
            scores[h] = score.astype(BF16)

        def attend_block(h):
            att[:, head(h)] = dot(scores[h], v_ref[:, head(h)], 1, 0)

        def attend_prior(h):
            att[:, head(h)] = att[:, head(h)] + dot_wide(q_ref[:, head(h)], prior[h], 1, 0)

        counted = set()

        def count(i, out, weighted):
            square, cross = out * out, weighted * out
            squares[i] = squares[i] + square if i in counted else square
            crossed[i] = crossed[i] + cross if i in counted else cross
            counted.add(i)

        def add_stats(h):
            count(0, att[:, head(h)], g_ref[:, head(h)].astype(F32) * gain_ref[h:h + 1, :])

        def send_early(h, first, slots, target, state=None):
            early_out[first] = q_ref[:, head(h)].astype(F32)
            send(move_early(first, slots, target))
            early_out[first + 1] = g_ref[:, head(h)].astype(F32)
            send(move_early(first + 1, slots + 1, target))
            score_of(h)
            local = dot(scores[h], v_ref[:, head(h)], 1, 0)
            att[:, head(h)] = local
            if state is not None:
                early_arrive(state, 2)
                local = local + dot_wide(q_ref[:, head(h)], early_in[state], 1, 0)
            early_out[first + 2] = local
            send(move_early(first + 2, slots + 2, target))

        def help_attend(j, first, h, state, i):
            for n in range(first, first + 3):
                early_arrive(n, own + max(i, 1))
            out = early_in[first + 2] + dot_wide(early_in[first].astype(BF16), state, 1, 0)
            help_att[j] = out
            if i:
                count(i, out, early_in[first + 1] * gain_ref[h:h + 1, :])

        def help_back(j, first, h, factors):
            scaled = early_in[first + 1] * factors[0]
            grad = (gain_ref[h:h + 1, :] * scaled - help_att[j] * factors[1]).astype(BF16)
            return dot(early_in[first].astype(BF16), grad, 0, 0)

        def relay(mine, come, move, order, slots, start=True):
            slots = list(slots)
            for h in order:
                for p in range(PIECES):
                    move(h, p).wait_recv()
                    mine[h, part(p)] = mine[h, part(p)] + come[h, part(p)]
                    send(move(h, p))
                    if slots:
                        slots.pop(0)()
            for step in slots:
                step()

        def put_stats():
            for i in sorted(counted):
                b = 2 * (own + i)
                stat[slot, b:b + 1, :] = jnp.sum(squares[i].T, axis=0, keepdims=True)
                stat[slot, b + 1:b + 2, :] = jnp.sum(crossed[i].T, axis=0, keepdims=True)

        def stat_move(n, target, i):
            return pltpu.make_async_remote_copy(
                src_ref=stat.at[slot], dst_ref=stat.at[slot],
                send_sem=stat_send.at[n], recv_sem=stat_recv.at[slot],
                device_id={"seq": target, "tp": tp_peer(i)}, device_id_type=MESH,
            )

        def send_stats():
            n = 0
            for target in ((0,), (1, 3, 2), (2, 3, 1), (3, 2, 1))[own]:
                for i in range(1 if target == own else 0, n_tp):
                    send(stat_move(n, target, i))
                    n += 1

        def sum_stats(source):
            for i in range(1 if source == own else 0, n_tp):
                s = source * n_tp + tp_peer(i)
                pltpu.make_async_remote_copy(
                    src_ref=stat.at[s], dst_ref=stat.at[s],
                    send_sem=stat_send.at[0], recv_sem=stat_recv.at[s],
                    device_id={"tp": tp_peer(1)}, device_id_type=MESH,
                ).wait_recv()
            total_stat = stat[source * n_tp]
            for i in range(1, n_tp):
                total_stat = total_stat + stat[source * n_tp + i]
            return total_stat

        def factors_of(sums, b):
            scale = lax.rsqrt(sums[2 * b:2 * b + 1] / HID + EPSILON)
            factor = scale * scale * scale * sums[2 * b + 1:2 * b + 2] / HID
            return tuple(jnp.broadcast_to(x, (HD, rows)).T for x in (scale, factor))

        def upstream(h, factors):
            out = att[:, head(h)]
            scaled = g_ref[:, head(h)].astype(F32) * factors[0]
            up[:, head(h)] = (gain_ref[h:h + 1, :] * scaled - out * factors[1]).astype(BF16)
            gain_seq[own, h:h + 1, :] = jnp.sum(scaled * out, axis=0, keepdims=True)

        def back_state(h):
            total_back[h] = dot(q_ref[:, head(h)], up[:, head(h)], 0, 0)

        def send_down(h):
            for p in range(PIECES):
                send(move_down(h, p))

        def gain_to_first(source):
            return pltpu.make_async_remote_copy(
                src_ref=gain_seq.at[source], dst_ref=gain_seq.at[source],
                send_sem=gs_send.at[source], recv_sem=gs_recv.at[source],
                device_id={"seq": 0}, device_id_type=MESH,
            )

        def gain_from_first(target):
            return pltpu.make_async_remote_copy(
                src_ref=gg, dst_ref=gain_back,
                send_sem=gb_send.at[target], recv_sem=gb_recv.at[target],
                device_id={"seq": target}, device_id_type=MESH,
            )

        def normed_of(h, factors):
            normed_out[:, head(h)] = (
                att[:, head(h)] * factors[0] * gain_ref[h:h + 1, :]
            ).astype(BF16)

        def mixed_of(h):
            mix = jnp.where(causal, dot(up[:, head(h)], v_ref[:, head(h)], 1, 1), 0.0)
            mixed[h] = mix.astype(BF16)

        def dq_of(h):
            wide = dot(mixed[h], k_ref[:, head(h)], 1, 0)
            if own > 0:
                wide = wide + dot_wide(up[:, head(h)], prior[h], 1, 1)
            dq_out[:, head(h)] = wide.astype(BF16)

        def block_parts(h):
            dk_part[h] = dot(mixed[h], q_ref[:, head(h)], 0, 0)
            dv_part[h] = dot(scores[h], up[:, head(h)], 0, 0)

        def dk_of(h):
            wide = dk_part[h]
            if own < 3:
                wide = wide + dot_wide(v_ref[:, head(h)], later[h], 1, 1)
            dk_out[:, head(h)] = wide.astype(BF16)

        def dv_of(h):
            wide = dv_part[h]
            if own < 3:
                wide = wide + dot_wide(k_ref[:, head(h)], later[h], 1, 0)
            dv_out[:, head(h)] = wide.astype(BF16)

        def local_work(h, factors):
            return [
                functools.partial(mixed_of, h),
                functools.partial(dq_of, h),
                functools.partial(block_parts, h),
                functools.partial(normed_of, h, factors),
            ]

        def last_work(h):
            return [functools.partial(dk_of, h), functools.partial(dv_of, h)]

        def run(steps):
            for step in steps:
                step()

        def local_attention(order):
            for h in order:
                score_of(h)
                attend_block(h)

        def own_part(h):
            return [functools.partial(attend_prior, h), functools.partial(add_stats, h)]

        def forward_slots(order):
            slots = [lambda: None] * PIECES
            for h in order:
                slots += own_part(h) + [lambda: None] * (PIECES - 2)
            return slots

        stat[slot] = jnp.zeros_like(stat[slot])
        for load in loads:
            load.wait()

        if own == 0:
            for h in range(heads):
                total_of(h)
                if h == 0:
                    pl.semaphore_wait(barrier, heard)
                for p in range(PIECES):
                    send(move_up(h, p))
            local_attention(range(heads))
            for h in range(heads):
                add_stats(h)
            put_stats()
            send_stats()
            factors = factors_of(sum_stats(0), 0)
            for h in range(heads):
                upstream(h, factors)
            for h in range(heads):
                run(local_work(h, factors))
            gains = [{"dp": lax.rem(d + i, n_dp)} for i in range(1, n_dp)]
            gain_moves = [
                pltpu.make_async_remote_copy(
                    src_ref=gain_dp.at[d], dst_ref=gain_dp.at[d],
                    send_sem=gd_send.at[i], recv_sem=gd_recv.at[i],
                    device_id=peer, device_id_type=MESH,
                )
                for i, peer in enumerate(gains)
            ]
            for n, h in enumerate(order_down):
                arrive(move_down, h)
                run(last_work(h))
                if n == 0:
                    for source in range(1, 4):
                        gain_to_first(source).wait_recv()
                    gain_dp[d] = (gain_seq[0] + gain_seq[1]) + (gain_seq[2] + gain_seq[3])
                    for move in gain_moves:
                        send(move)
                if n == 2:
                    for move in gain_moves:
                        move.wait_recv()
                    gain_sum = gain_dp[0]
                    for i in range(1, n_dp):
                        gain_sum = gain_sum + gain_dp[i]
                    gg[...] = gain_sum
                    for target in range(1, 4):
                        send(gain_from_first(target))
                    gg_out[...] = gain_sum

        if own == 1:
            pl.semaphore_wait(barrier, heard)
            for h in range(heads):
                total_of(h)
            local_attention(range(heads))
            relay(total, prior, move_up, range(heads), forward_slots(range(heads)))
            help_attend(0, 3, far, total[far], 1)
            help_attend(1, 0, far, total[far], 2)
            put_stats()
            send_stats()
            sums = sum_stats(1)
            factors = factors_of(sums, 1)
            for h in order_down:
                upstream(h, factors)
                back_state(h)
            send(gain_to_first(own))
            run(local_work(far, factors))
            sums = sums + sum_stats(2)
            beyond = help_back(0, 3, far, factors_of(sums, 2))
            total_back[far] = total_back[far] + beyond
            sums = sums + sum_stats(3)
            last = help_back(1, 0, far, factors_of(sums, 3))
            total_back[far] = total_back[far] + last
            send_down(far)
            later[far] = beyond + last
            run(last_work(far))
            steps = []
            for h in near + common:
                steps += local_work(h, factors)
            run(steps[:2])
            relay(total_back, later, move_down, near + common, steps[2:])
            for h in near + common:
                run(last_work(h))

        if own == 2:
            total_of(far)
            early_out[3] = total[far]
            pl.semaphore_wait(barrier, heard)
            send(move_early(3, 0, 3))
            send_early(far, 0, 3, 1)
            for h in range(heads - 1):
                total_of(h)
            local_attention(range(heads - 1))
            relay(total, prior, move_up, range(heads - 1), forward_slots(range(heads - 2)))
            run(own_part(near[0]))
            help_attend(0, 0, near[0], total[near[0]], 1)
            help_attend(1, 3, near[1], total[near[1]], 1)
            put_stats()
            send_stats()
            relay(total, prior, move_up, (far,), ())
            attend_prior(far)
            sums = sum_stats(1) + sum_stats(2)
            factors = factors_of(sums, 2)
            for h in near:
                upstream(h, factors)
                back_state(h)
            sums = sums + sum_stats(3)
            ahead = factors_of(sums, 3)
            for j, h in enumerate(near):
                beyond = help_back(j, 3 * j, h, ahead)
                total_back[h] = total_back[h] + beyond
                send_down(h)
                later[h] = beyond
            for h in common:
                upstream(h, factors)
                back_state(h)
            upstream(far, factors)
            send(gain_to_first(own))
            steps = []
            for h in near:
                steps += local_work(h, factors) + last_work(h)
            for h in common + (far,):
                steps += local_work(h, factors)
            relay(total_back, later, move_down, common, steps)
            for h in common:
                run(last_work(h))
            arrive(move_down, far)
            run(last_work(far))

        if own == 3:
            pl.semaphore_wait(barrier, heard)
            send_early(near[0], 3, 0, 2)
            send_early(far, 0, 0, 1, 0)
            send_early(near[1], 6, 3, 2)
            local_attention(common)
            for h in common:
                arrive(move_up, h)
                attend_prior(h)
                add_stats(h)
            put_stats()
            send_stats()
            arrive(move_up, near[1])
            attend_prior(near[1])
            sums = sum_stats(1) + sum_stats(2)
            sums = sums + sum_stats(3)
            factors = factors_of(sums, 3)
            for h in common:
                upstream(h, factors)
                back_state(h)
                send_down(h)
            for h in (near[0], far):
                arrive(move_up, h)
                attend_prior(h)
            for h in near + (far,):
                upstream(h, factors)
            send(gain_to_first(own))
            back_state(far)
            send_down(far)
            for h in range(heads):
                run(local_work(h, factors))
                run(last_work(h))

        if own > 0:
            gain_from_first(own).wait_recv()
            gg_out[...] = gain_back[...]
        for move in sent:
            move.wait_send()

    for own in range(4):
        pl.when(z == own)(functools.partial(program, own))


def write_out(*refs):
    copies = [pltpu.make_async_copy(refs[i], refs[5 + i], refs[10].at[i]) for i in range(5)]
    for copy in copies:
        copy.start()
    for copy in copies:
        copy.wait()


def solution(mesh):
    n_seq, n_tp, n_dp = (mesh.shape[name] for name in ("seq", "tp", "dp"))

    def local(queries, keys, values, out_gain, grad_out):
        shape = queries.shape
        rows, width = shape[0] * shape[1], shape[2]
        heads = width // HD
        chunks = heads * PIECES
        matrix = jax.ShapeDtypeStruct((rows, width), BF16)
        state = pltpu.VMEM((heads, HD, HD), F32)
        page = pltpu.VMEM((rows, width), BF16)
        tile = lambda *lead: pltpu.VMEM((*lead, rows, HD), F32)
        sems = pltpu.SemaphoreType.DMA
        flat = lambda x: x.reshape(rows, width)
        with_help = n_seq == 4 and rows == HD and heads >= 4
        if with_help:
            body = functools.partial(helped, n_tp, n_dp)
            sums, stats = tile(3), n_seq * n_tp
            early = [tile(9), tile(6), tile(2)]
            early_sems = [sems((9,)), sems((6,))]
            pages, out_sems, out_space = [], [], pltpu.VMEM
            stat_sems = [sems((3 * n_tp,)), sems((n_seq * n_tp,))]
        else:
            body = functools.partial(kernel, n_seq, n_tp, n_dp)
            sums, stats, early, early_sems = tile(), n_tp, [], []
            pages, out_sems, out_space = [page] * 4, [sems((4 * heads + 1,))], pl.ANY
            stat_sems = [sems((max(n_tp - 1, 1),)), sems((max(n_tp - 1, 1),))]
        outs = pl.pallas_call(
            body,
            out_shape=(matrix,) * 4 + (jax.ShapeDtypeStruct((heads, HD), F32),),
            in_specs=[pl.BlockSpec(memory_space=pltpu.HBM)] * 5,
            out_specs=[pl.BlockSpec(memory_space=out_space)] * 5,
            scratch_shapes=[
                page, page, page, pltpu.VMEM((heads, HD), F32), page,
                state, state, state, state,
                pltpu.VMEM((rows, width), F32),
                pltpu.VMEM((heads, rows, rows), BF16), pltpu.VMEM((heads, rows, rows), BF16),
                sums, sums, tile(heads), tile(heads),
                page, *pages,
                *early,
                pltpu.VMEM((stats, 8, rows), F32),
                pltpu.VMEM((n_seq, heads, HD), F32),
                pltpu.VMEM((n_dp, heads, HD), F32),
                pltpu.VMEM((heads, HD), F32), pltpu.VMEM((heads, HD), F32),
                sems((5,)), *out_sems,
                sems((chunks,)), sems((chunks,)), sems((chunks,)), sems((chunks,)),
                *early_sems,
                *stat_sems,
                sems((n_seq,)), sems((n_seq,)),
                sems((max(n_dp - 1, 1),)), sems((max(n_dp - 1, 1),)),
                sems((n_seq,)), sems((n_seq,)),
            ],
            compiler_params=pltpu.CompilerParams(
                collective_id=0, has_side_effects=True, vmem_limit_bytes=32 << 20
            ),
        )(
            *(
                pltpu.with_memory_space_constraint(x, pltpu.HBM)
                for x in (
                    flat(queries), flat(keys), flat(values),
                    out_gain.reshape(heads, HD), flat(grad_out),
                )
            )
        )
        outs = pl.pallas_call(
            write_out,
            out_shape=tuple(jax.ShapeDtypeStruct(x.shape, x.dtype) for x in outs),
            in_specs=[pl.BlockSpec(memory_space=pl.ANY)] * 5,
            out_specs=[pl.BlockSpec(memory_space=pl.ANY)] * 5,
            scratch_shapes=[sems((5,))],
            compiler_params=pltpu.CompilerParams(vmem_limit_bytes=8 << 20),
        )(*outs)
        return tuple(x.reshape(shape) for x in outs[:4]) + (outs[4].reshape(width),)

    spec = P("dp", "seq", "tp")
    return jax.shard_map(
        local,
        mesh=mesh,
        in_specs=(spec, spec, spec, P("tp"), spec),
        out_specs=(spec, spec, spec, spec, P("tp")),
        check_vma=False,
    )
```

```python
import functools

import jax
import jax.numpy as jnp
from jax import lax
from jax.experimental import pallas as pl
from jax.experimental.pallas import tpu as pltpu
from jax.sharding import PartitionSpec as P

HD = 128
HID = 4096
EPSILON = 1e-06
PIECES = 4
PART = HD // PIECES
MESH = pl.DeviceIdType.MESH
F32 = jnp.float32
BF16 = jnp.bfloat16


def dot(a, b, ca, cb):
    return lax.dot_general(a, b, (((ca,), (cb,)), ((), ())), preferred_element_type=F32)


def split(x):
    high = x.astype(BF16)
    return high, (x - high.astype(F32)).astype(BF16)


def dot_wide(a, x, ca, cb):
    both = jnp.concatenate(split(x), axis=cb)
    return dot(jnp.concatenate((a, a), axis=ca), both, ca, cb)


def kernel(
    n_seq, n_tp, n_dp,
    q_in, k_in, v_in, gain_in, g_in,
    normed_out, dq_out, dk_out, dv_out, gg_out,
    q_ref, k_ref, v_ref, gain_ref, g_ref,
    prior, total, later, total_back,
    att, scores, mixed, squares, crossed, dk_part, dv_part, up, normed, dq, dk, dv,
    stat, gain_seq, gain_dp, gg, gain_back,
    in_sem, out_sem,
    up_send, up_recv, down_send, down_recv,
    stat_send, stat_recv, gs_send, gs_recv, gd_send, gd_recv,
    gb_send, gb_recv,
):
    rows, width = q_ref.shape
    heads = width // HD
    z = lax.axis_index("seq")
    t = lax.axis_index("tp")
    d = lax.axis_index("dp")
    first, last = z == 0, z == n_seq - 1
    above = lax.rem(z + 1, n_seq)
    below = lax.rem(z + n_seq - 1, n_seq)

    def head(h):
        return slice(h * HD, (h + 1) * HD)

    def peers(axis, me, size):
        return [{axis: lax.rem(me + i, size)} for i in range(1, size)]

    greeted = peers("tp", t, n_tp) + peers("dp", d, n_dp)
    if n_seq > 1:
        greeted.append({"seq": below})
    barrier = pltpu.get_barrier_semaphore()
    for peer in greeted:
        pl.semaphore_signal(barrier, inc=1, device_id=peer, device_id_type=MESH)

    loads = [
        pltpu.make_async_copy(src, dst, in_sem.at[i])
        for i, (src, dst) in enumerate(
            [(k_in, k_ref), (v_in, v_ref), (q_in, q_ref), (g_in, g_ref), (gain_in, gain_ref)]
        )
    ]
    for load in loads:
        load.start()
    loads[0].wait()
    loads[1].wait()

    def part(p):
        return slice(p * PART, (p + 1) * PART)

    def move_up(h, p):
        i = h * PIECES + p
        return pltpu.make_async_remote_copy(
            src_ref=total.at[h, part(p)], dst_ref=prior.at[h, part(p)],
            send_sem=up_send.at[i], recv_sem=up_recv.at[i],
            device_id={"seq": above}, device_id_type=MESH,
        )

    def move_down(h, p):
        i = h * PIECES + p
        return pltpu.make_async_remote_copy(
            src_ref=total_back.at[h, part(p)], dst_ref=later.at[h, part(p)],
            send_sem=down_send.at[i], recv_sem=down_recv.at[i],
            device_id={"seq": below}, device_id_type=MESH,
        )

    def relay(h, p, mine, come, move, is_first, is_last):
        @pl.when(jnp.logical_and(jnp.logical_not(is_first), jnp.logical_not(is_last)))
        def _():
            move(h, p).wait_recv()
            mine[h, part(p)] = mine[h, part(p)] + come[h, part(p)]
            move(h, p).start()

        @pl.when(jnp.logical_and(is_last, jnp.logical_not(is_first)))
        def _():
            move(h, p).wait_recv()

    def relay_all(mine, come, move, is_first, is_last, slots):
        for h in range(heads):
            for p in range(PIECES):
                relay(h, p, mine, come, move, is_first, is_last)
                for step in slots[h * PIECES + p]:
                    step()

    for h in range(heads):
        total[h] = dot(k_ref[:, head(h)], v_ref[:, head(h)], 0, 0)
        if h == 0:
            pl.semaphore_wait(barrier, len(greeted))
        if n_seq > 1:
            @pl.when(first)
            def _():
                for p in range(PIECES):
                    move_up(h, p).start()

    @pl.when(first)
    def _():
        prior[...] = jnp.zeros_like(prior)

    @pl.when(last)
    def _():
        later[...] = jnp.zeros_like(later)

    loads[2].wait()
    loads[3].wait()
    loads[4].wait()
    causal = lax.broadcasted_iota(jnp.int32, (rows, rows), 0) >= lax.broadcasted_iota(
        jnp.int32, (rows, rows), 1
    )
    def score_of(h):
        score = jnp.where(causal, dot(q_ref[:, head(h)], k_ref[:, head(h)], 1, 1), 0.0)
        scores[h] = score.astype(BF16)

    def attend_block(h):
        att[:, head(h)] = dot(scores[h], v_ref[:, head(h)], 1, 0)

    def attend_prior(h):
        att[:, head(h)] = att[:, head(h)] + dot_wide(q_ref[:, head(h)], prior[h], 1, 0)

    def add_stats(h):
        out = att[:, head(h)]
        square = out * out
        cross = g_ref[:, head(h)].astype(F32) * gain_ref[h:h + 1, :] * out
        squares[...] = square if h == 0 else squares[...] + square
        crossed[...] = cross if h == 0 else crossed[...] + cross

    slots = [[] for _ in range(heads * PIECES)]
    for h in range(heads):
        slots[h * PIECES].append(functools.partial(score_of, h))
        slots[h * PIECES + 1].append(functools.partial(attend_block, h))
        if h > 0:
            slots[h * PIECES + 2].append(functools.partial(attend_prior, h - 1))
            slots[h * PIECES + 3].append(functools.partial(add_stats, h - 1))
    relay_all(total, prior, move_up, first, last, slots)
    attend_prior(heads - 1)
    add_stats(heads - 1)

    stat[t, 0:1, :] = jnp.sum(squares[...].T, axis=0, keepdims=True)
    stat[t, 1:2, :] = jnp.sum(crossed[...].T, axis=0, keepdims=True)

    def all_send(buffer, axis, me, size, send, recv):
        return [
            pltpu.make_async_remote_copy(
                src_ref=buffer.at[me], dst_ref=buffer.at[me],
                send_sem=send.at[i - 1], recv_sem=recv.at[i - 1],
                device_id={axis: lax.rem(me + i, size)}, device_id_type=MESH,
            )
            for i in range(1, size)
        ]

    stat_moves = all_send(stat, "tp", t, n_tp, stat_send, stat_recv)
    for move in stat_moves:
        move.start()
    for move in stat_moves:
        move.wait_recv()
    sums = stat[0, 0:2, :]
    for i in range(1, n_tp):
        sums = sums + stat[i, 0:2, :]
    scale_row = lax.rsqrt(sums[0:1] / HID + EPSILON)
    factor_row = scale_row * scale_row * scale_row * sums[1:2] / HID
    scale = jnp.broadcast_to(scale_row, (HD, rows)).T
    factor = jnp.broadcast_to(factor_row, (HD, rows)).T

    def upstream(h):
        out = att[:, head(h)]
        grad = g_ref[:, head(h)].astype(F32)
        scaled = grad * scale
        up[:, head(h)] = (gain_ref[h:h + 1, :] * scaled - out * factor).astype(BF16)
        gain_seq[z, h:h + 1, :] = jnp.sum(scaled * out, axis=0, keepdims=True)

    def back_state(h):
        total_back[h] = dot(q_ref[:, head(h)], up[:, head(h)], 0, 0)
        if n_seq > 1:
            @pl.when(last)
            def _():
                for p in range(PIECES):
                    move_down(h, p).start()

    upstream(0)
    back_state(0)
    for h in range(1, heads):
        upstream(h)

    def gain_to_first(source):
        return pltpu.make_async_remote_copy(
            src_ref=gain_seq.at[source], dst_ref=gain_seq.at[source],
            send_sem=gs_send.at[source], recv_sem=gs_recv.at[source],
            device_id={"seq": 0}, device_id_type=MESH,
        )

    def gain_from_first(target):
        return pltpu.make_async_remote_copy(
            src_ref=gg, dst_ref=gain_back,
            send_sem=gb_send.at[target], recv_sem=gb_recv.at[target],
            device_id={"seq": target}, device_id_type=MESH,
        )

    @pl.when(jnp.logical_not(first))
    def _():
        gain_to_first(z).start()

    for h in range(1, heads):
        back_state(h)

    dp_moves = all_send(gain_dp, "dp", d, n_dp, gd_send, gd_recv)
    stores = []

    def store(src, dst):
        copy = pltpu.make_async_copy(src, dst, out_sem.at[len(stores)])
        copy.start()
        stores.append(copy)

    def normed_of(h):
        normed[:, head(h)] = (att[:, head(h)] * scale * gain_ref[h:h + 1, :]).astype(BF16)
        store(normed.at[:, head(h)], normed_out.at[:, head(h)])

    def mixed_of(h):
        mix = jnp.where(causal, dot(up[:, head(h)], v_ref[:, head(h)], 1, 1), 0.0)
        mixed[h] = mix.astype(BF16)

    def dq_of(h):
        dq[:, head(h)] = (
            dot(mixed[h], k_ref[:, head(h)], 1, 0) + dot_wide(up[:, head(h)], prior[h], 1, 1)
        ).astype(BF16)
        store(dq.at[:, head(h)], dq_out.at[:, head(h)])

    def block_parts(h):
        dk_part[h] = dot(mixed[h], q_ref[:, head(h)], 0, 0)
        dv_part[h] = dot(scores[h], up[:, head(h)], 0, 0)

    def dk_of(h):
        wide = dot_wide(v_ref[:, head(h)], later[h], 1, 1)
        dk[:, head(h)] = (dk_part[h] + wide).astype(BF16)
        store(dk.at[:, head(h)], dk_out.at[:, head(h)])

    def dv_of(h):
        wide = dot_wide(k_ref[:, head(h)], later[h], 1, 0)
        dv[:, head(h)] = (dv_part[h] + wide).astype(BF16)
        store(dv.at[:, head(h)], dv_out.at[:, head(h)])

    def gain_middle():
        @pl.when(first)
        def _():
            for source in range(1, n_seq):
                gain_to_first(source).wait_recv()
            gain_sum = gain_seq[0]
            for i in range(1, n_seq):
                gain_sum = gain_sum + gain_seq[i]
            gain_dp[d] = gain_sum
            for move in dp_moves:
                move.start()

    def gain_end():
        @pl.when(first)
        def _():
            for move in dp_moves:
                move.wait_recv()
            gain_sum = gain_dp[0]
            for i in range(1, n_dp):
                gain_sum = gain_sum + gain_dp[i]
            gg[...] = gain_sum
            for target in range(1, n_seq):
                gain_from_first(target).start()

    block_work = [
        functools.partial(work, h)
        for h in range(heads)
        for work in (mixed_of, dq_of, block_parts, normed_of)
    ]
    half = 2 * heads
    for step in block_work[:half]:
        step()
    slots = [[] for _ in range(heads * PIECES)]
    for h in range(heads):
        if h > 0:
            slots[h * PIECES].append(functools.partial(dk_of, h - 1))
            slots[h * PIECES + 1].append(functools.partial(dv_of, h - 1))
        slots[h * PIECES + 2].append(block_work[half + 2 * h])
        slots[h * PIECES + 3].append(block_work[half + 2 * h + 1])
    slots[0].append(gain_middle)
    slots[heads // 4 * PIECES].append(gain_end)
    relay_all(total_back, later, move_down, last, first, slots)
    dk_of(heads - 1)
    dv_of(heads - 1)

    gg_copy = pltpu.make_async_copy(gg, gg_out, out_sem.at[4 * heads])

    @pl.when(first)
    def _():
        gg_copy.start()
        for move in dp_moves:
            move.wait_send()
        for target in range(1, n_seq):
            gain_from_first(target).wait_send()

    back_copy = pltpu.make_async_copy(gain_back, gg_out, out_sem.at[4 * heads])

    @pl.when(jnp.logical_not(first))
    def _():
        gain_from_first(z).wait_recv()
        back_copy.start()
        gain_to_first(z).wait_send()

    for move in stat_moves:
        move.wait_send()
    if n_seq > 1:
        @pl.when(jnp.logical_not(last))
        def _():
            for h in range(heads):
                for p in range(PIECES):
                    move_up(h, p).wait_send()

        @pl.when(jnp.logical_not(first))
        def _():
            for h in range(heads):
                for p in range(PIECES):
                    move_down(h, p).wait_send()
    for copy in stores:
        copy.wait()

    @pl.when(first)
    def _():
        gg_copy.wait()

    @pl.when(jnp.logical_not(first))
    def _():
        back_copy.wait()


def helped(
    n_tp, n_dp,
    q_in, k_in, v_in, gain_in, g_in,
    normed_out, dq_out, dk_out, dv_out, gg_out,
    q_ref, k_ref, v_ref, gain_ref, g_ref,
    prior, total, later, total_back,
    att, scores, mixed, squares, crossed, dk_part, dv_part, up,
    early_out, early_in, help_att,
    stat, gain_seq, gain_dp, gg, gain_back,
    in_sem,
    up_send, up_recv, down_send, down_recv,
    early_send, early_recv,
    stat_send, stat_recv, gs_send, gs_recv, gd_send, gd_recv,
    gb_send, gb_recv, pace,
):
    rows, width = q_ref.shape
    heads = width // HD
    far, near = heads - 1, (heads - 2, heads - 3)
    common = tuple(range(heads - 3))
    order_down = (far,) + near + common
    z = lax.axis_index("seq")
    t = lax.axis_index("tp")
    d = lax.axis_index("dp")
    slot = z * n_tp + t

    def head(h):
        return slice(h * HD, (h + 1) * HD)

    def part(p):
        return slice(p * PART, (p + 1) * PART)

    def tp_peer(i):
        return lax.rem(t + i, n_tp)

    causal = lax.broadcasted_iota(jnp.int32, (rows, rows), 0) >= lax.broadcasted_iota(
        jnp.int32, (rows, rows), 1
    )
    loads = [
        pltpu.make_async_copy(src, dst, in_sem.at[i])
        for i, (src, dst) in enumerate(
            [(k_in, k_ref), (v_in, v_ref), (q_in, q_ref), (g_in, g_ref), (gain_in, gain_ref)]
        )
    ]

    def program(own):
        barrier = pltpu.get_barrier_semaphore()
        greeted = [{"tp": tp_peer(i)} for i in range(1, n_tp)]
        heard = len(greeted)
        if own == 0:
            greeted += [{"dp": lax.rem(d + i, n_dp)} for i in range(1, n_dp)]
            heard = len(greeted) + 1
        else:
            heard += 2
        greeted += [{"seq": i} for i in ((1,), (0, 2, 3), (1, 3), (2,))[own]]
        for peer in greeted:
            pl.semaphore_signal(barrier, inc=1, device_id=peer, device_id_type=MESH)
        for load in loads:
            load.start()

        sent = []

        def send(move):
            move.start()
            sent.append(move)

        def move_up(h, p):
            i = h * PIECES + p
            return pltpu.make_async_remote_copy(
                src_ref=total.at[h, part(p)], dst_ref=prior.at[h, part(p)],
                send_sem=up_send.at[i], recv_sem=up_recv.at[i],
                device_id={"seq": min(own + 1, 3)}, device_id_type=MESH,
            )

        def move_down(h, p):
            i = h * PIECES + p
            return pltpu.make_async_remote_copy(
                src_ref=total_back.at[h, part(p)], dst_ref=later.at[h, part(p)],
                send_sem=down_send.at[i], recv_sem=down_recv.at[i],
                device_id={"seq": max(own - 1, 0)}, device_id_type=MESH,
            )

        def arrive(move, h):
            for p in range(PIECES):
                move(h, p).wait_recv()

        def move_early(i, j, target):
            return pltpu.make_async_remote_copy(
                src_ref=early_out.at[i], dst_ref=early_in.at[j],
                send_sem=early_send.at[i], recv_sem=early_recv.at[j],
                device_id={"seq": target}, device_id_type=MESH,
            )

        def early_arrive(j, source):
            move_early(0, j, source).wait_recv()

        def total_of(h):
            total[h] = dot(k_ref[:, head(h)], v_ref[:, head(h)], 0, 0)

        def score_of(h):
            score = jnp.where(causal, dot(q_ref[:, head(h)], k_ref[:, head(h)], 1, 1), 0.0)
            scores[h] = score.astype(BF16)

        def attend_block(h):
            att[:, head(h)] = dot(scores[h], v_ref[:, head(h)], 1, 0)

        def attend_prior(h):
            att[:, head(h)] = att[:, head(h)] + dot_wide(q_ref[:, head(h)], prior[h], 1, 0)

        counted = set()

        def count(i, out, weighted):
            square, cross = out * out, weighted * out
            squares[i] = squares[i] + square if i in counted else square
            crossed[i] = crossed[i] + cross if i in counted else cross
            counted.add(i)

        def add_stats(h):
            count(0, att[:, head(h)], g_ref[:, head(h)].astype(F32) * gain_ref[h:h + 1, :])

        def send_early(h, first, slots, target, state=None):
            early_out[first] = q_ref[:, head(h)].astype(F32)
            send(move_early(first, slots, target))
            early_out[first + 1] = g_ref[:, head(h)].astype(F32)
            send(move_early(first + 1, slots + 1, target))
            score_of(h)
            local = dot(scores[h], v_ref[:, head(h)], 1, 0)
            att[:, head(h)] = local
            if state is not None:
                early_arrive(state, 2)
                local = local + dot_wide(q_ref[:, head(h)], early_in[state], 1, 0)
            early_out[first + 2] = local
            send(move_early(first + 2, slots + 2, target))

        def help_attend(j, first, h, state, i):
            early_arrive(first, own + i)
            wide = dot_wide(early_in[first].astype(BF16), state, 1, 0)
            for n in (first + 1, first + 2):
                early_arrive(n, own + i)
            out = early_in[first + 2] + wide
            help_att[j] = out
            count(i, out, early_in[first + 1] * gain_ref[h:h + 1, :])

        def help_back(j, first, h, factors):
            scaled = early_in[first + 1] * factors[0]
            grad = (gain_ref[h:h + 1, :] * scaled - help_att[j] * factors[1]).astype(BF16)
            return dot(early_in[first].astype(BF16), grad, 0, 0)

        def relay(mine, come, move, order, slots, start=True):
            slots = list(slots)
            for h in order:
                for p in range(PIECES):
                    move(h, p).wait_recv()
                    mine[h, part(p)] = mine[h, part(p)] + come[h, part(p)]
                    send(move(h, p))
                    if slots:
                        slots.pop(0)()
            for step in slots:
                step()

        def put_stats(blocks):
            for i in blocks:
                b = 2 * (own + i)
                stat[slot, b:b + 1, :] = jnp.sum(squares[i].T, axis=0, keepdims=True)
                stat[slot, b + 1:b + 2, :] = jnp.sum(crossed[i].T, axis=0, keepdims=True)

        def stat_move(n, target, i):
            return pltpu.make_async_remote_copy(
                src_ref=stat.at[slot], dst_ref=stat.at[slot],
                send_sem=stat_send.at[n], recv_sem=stat_recv.at[slot],
                device_id={"seq": target, "tp": tp_peer(i)}, device_id_type=MESH,
            )

        def send_stats():
            n = 0
            for target in ((0,), (1, 3, 2), (2, 3, 1), (3, 2, 1))[own]:
                for i in range(1 if target == own else 0, n_tp):
                    send(stat_move(n, target, i))
                    n += 1

        def sum_stats(source):
            for i in range(1 if source == own else 0, n_tp):
                s = source * n_tp + tp_peer(i)
                pltpu.make_async_remote_copy(
                    src_ref=stat.at[s], dst_ref=stat.at[s],
                    send_sem=stat_send.at[0], recv_sem=stat_recv.at[s],
                    device_id={"tp": tp_peer(1)}, device_id_type=MESH,
                ).wait_recv()
            total_stat = stat[source * n_tp]
            for i in range(1, n_tp):
                total_stat = total_stat + stat[source * n_tp + i]
            return total_stat

        def factors_of(sums, b):
            scale = lax.rsqrt(sums[2 * b:2 * b + 1] / HID + EPSILON)
            factor = scale * scale * scale * sums[2 * b + 1:2 * b + 2] / HID
            return tuple(jnp.broadcast_to(x, (HD, rows)).T for x in (scale, factor))

        def upstream(h, factors):
            out = att[:, head(h)]
            scaled = g_ref[:, head(h)].astype(F32) * factors[0]
            up[:, head(h)] = (gain_ref[h:h + 1, :] * scaled - out * factors[1]).astype(BF16)
            gain_seq[own, h:h + 1, :] = jnp.sum(scaled * out, axis=0, keepdims=True)

        def back_state(h):
            total_back[h] = dot(q_ref[:, head(h)], up[:, head(h)], 0, 0)

        def send_down(h):
            for p in range(PIECES):
                send(move_down(h, p))

        def gain_to_first(source):
            return pltpu.make_async_remote_copy(
                src_ref=gain_seq.at[source], dst_ref=gain_seq.at[source],
                send_sem=gs_send.at[source], recv_sem=gs_recv.at[source],
                device_id={"seq": 0}, device_id_type=MESH,
            )

        def gain_from_first(target):
            return pltpu.make_async_remote_copy(
                src_ref=gg, dst_ref=gain_back,
                send_sem=gb_send.at[target], recv_sem=gb_recv.at[target],
                device_id={"seq": target}, device_id_type=MESH,
            )

        def normed_of(h, factors):
            normed_out[:, head(h)] = (
                att[:, head(h)] * factors[0] * gain_ref[h:h + 1, :]
            ).astype(BF16)

        def mixed_of(h):
            mix = jnp.where(causal, dot(up[:, head(h)], v_ref[:, head(h)], 1, 1), 0.0)
            mixed[h] = mix.astype(BF16)

        def dq_of(h):
            wide = dot(mixed[h], k_ref[:, head(h)], 1, 0)
            if own > 0:
                wide = wide + dot_wide(up[:, head(h)], prior[h], 1, 1)
            dq_out[:, head(h)] = wide.astype(BF16)

        def block_parts(h):
            dk_part[h] = dot(mixed[h], q_ref[:, head(h)], 0, 0)
            dv_part[h] = dot(scores[h], up[:, head(h)], 0, 0)

        def dk_of(h):
            wide = dk_part[h]
            if own < 3:
                wide = wide + dot_wide(v_ref[:, head(h)], later[h], 1, 1)
            dk_out[:, head(h)] = wide.astype(BF16)

        def dv_of(h):
            wide = dv_part[h]
            if own < 3:
                wide = wide + dot_wide(k_ref[:, head(h)], later[h], 1, 0)
            dv_out[:, head(h)] = wide.astype(BF16)

        def local_work(h, factors):
            return [
                functools.partial(mixed_of, h),
                functools.partial(dq_of, h),
                functools.partial(block_parts, h),
                functools.partial(normed_of, h, factors),
            ]

        def last_work(h):
            return [functools.partial(dk_of, h), functools.partial(dv_of, h)]

        def run(steps):
            for step in steps:
                step()

        def local_attention(order):
            for h in order:
                score_of(h)
                attend_block(h)

        def own_part(h):
            return [functools.partial(attend_prior, h), functools.partial(add_stats, h)]

        def forward_slots(order):
            slots = [lambda: None] * PIECES
            for h in order:
                slots += own_part(h) + [lambda: None] * (PIECES - 2)
            return slots

        stat[slot] = jnp.zeros_like(stat[slot])
        for load in loads:
            load.wait()

        if own == 0:
            for h in range(heads):
                total_of(h)
                if h == 0:
                    pl.semaphore_wait(barrier, heard)
                if h in common:
                    for p in range(PIECES):
                        send(move_up(h, p))
            first_moves = list(sent)
            sent.clear()
            sent += [move_up(h, p) for h in range(heads - 3, heads) for p in range(PIECES)]
            odd = t % 2 == 1

            @pl.when(odd)
            def _():
                pl.semaphore_wait(pace, 1)
                for move in sent:
                    move.start()
                for move in first_moves:
                    move.wait_send()

            @pl.when(jnp.logical_not(odd))
            def _():
                for move in sent:
                    move.start()
                for move in first_moves[:-6]:
                    move.wait_send()
                pl.semaphore_signal(
                    pace, inc=1, device_id={"tp": t + 1}, device_id_type=MESH
                )
                for move in first_moves[-6:]:
                    move.wait_send()

            local_attention(range(heads))
            for h in range(heads):
                add_stats(h)
            put_stats((0,))
            send_stats()
            factors = factors_of(sum_stats(0), 0)
            for h in range(heads):
                upstream(h, factors)
            for h in range(heads):
                run(local_work(h, factors))
            gains = [{"dp": lax.rem(d + i, n_dp)} for i in range(1, n_dp)]
            gain_moves = [
                pltpu.make_async_remote_copy(
                    src_ref=gain_dp.at[d], dst_ref=gain_dp.at[d],
                    send_sem=gd_send.at[i], recv_sem=gd_recv.at[i],
                    device_id=peer, device_id_type=MESH,
                )
                for i, peer in enumerate(gains)
            ]
            for n, h in enumerate(order_down):
                arrive(move_down, h)
                run(last_work(h))
                if n == 0:
                    for source in range(1, 4):
                        gain_to_first(source).wait_recv()
                    gain_dp[d] = (gain_seq[0] + gain_seq[1]) + (gain_seq[2] + gain_seq[3])
                    for move in gain_moves:
                        send(move)
                if n == 2:
                    for move in gain_moves:
                        move.wait_recv()
                    gain_sum = gain_dp[0]
                    for i in range(1, n_dp):
                        gain_sum = gain_sum + gain_dp[i]
                    gg[...] = gain_sum
                    for target in range(1, 4):
                        send(gain_from_first(target))
                    gg_out[...] = gain_sum

        if own == 1:
            pl.semaphore_wait(barrier, heard)
            for h in range(heads):
                total_of(h)
            local_attention(range(heads))
            relay(total, prior, move_up, range(heads), forward_slots(range(heads)))
            help_attend(0, 3, far, total[far], 1)
            help_attend(1, 0, far, total[far], 2)
            put_stats((0, 1, 2))
            send_stats()
            sums = sum_stats(1)
            factors = factors_of(sums, 1)
            for h in order_down:
                upstream(h, factors)
                back_state(h)
            send(gain_to_first(own))
            run(local_work(far, factors))
            sums = sums + sum_stats(2)
            beyond = help_back(0, 3, far, factors_of(sums, 2))
            total_back[far] = total_back[far] + beyond
            sums = sums + sum_stats(3)
            last = help_back(1, 0, far, factors_of(sums, 3))
            total_back[far] = total_back[far] + last
            send_down(far)
            later[far] = beyond + last
            run(last_work(far))
            steps = []
            for h in near + common:
                steps += local_work(h, factors)
            run(steps[:2])
            relay(total_back, later, move_down, near + common, steps[2:])
            for h in near + common:
                run(last_work(h))

        if own == 2:
            total_of(far)
            early_out[3] = total[far]
            pl.semaphore_wait(barrier, heard)
            send(move_early(3, 0, 3))
            send_early(far, 0, 3, 1)
            for h in range(heads - 1):
                total_of(h)
            local_attention(range(heads - 1))
            relay(total, prior, move_up, range(heads - 1), forward_slots(range(heads - 2)))
            run(own_part(near[0]))
            help_attend(0, 0, near[0], total[near[0]], 1)
            put_stats((0,))
            help_attend(1, 3, near[1], total[near[1]], 1)
            put_stats((1,))
            send_stats()
            relay(total, prior, move_up, (far,), ())
            attend_prior(far)
            sums = sum_stats(1) + sum_stats(2)
            factors = factors_of(sums, 2)
            for h in near:
                upstream(h, factors)
                back_state(h)
            sums = sums + sum_stats(3)
            ahead = factors_of(sums, 3)
            for j, h in enumerate(near):
                beyond = help_back(j, 3 * j, h, ahead)
                total_back[h] = total_back[h] + beyond
                send_down(h)
                later[h] = beyond
            for h in common:
                upstream(h, factors)
                back_state(h)
            upstream(far, factors)
            send(gain_to_first(own))
            steps = []
            for h in near:
                steps += local_work(h, factors) + last_work(h)
            for h in common + (far,):
                steps += local_work(h, factors)
            relay(total_back, later, move_down, common, steps)
            for h in common:
                run(last_work(h))
            arrive(move_down, far)
            run(last_work(far))

        if own == 3:
            pl.semaphore_wait(barrier, heard)
            send_early(near[0], 3, 0, 2)
            send_early(far, 0, 0, 1, 0)
            send_early(near[1], 6, 3, 2)
            local_attention(common)
            for h in common:
                arrive(move_up, h)
                attend_prior(h)
                add_stats(h)
            put_stats((0,))
            send_stats()
            arrive(move_up, near[1])
            attend_prior(near[1])
            sums = sum_stats(1) + sum_stats(2)
            sums = sums + sum_stats(3)
            factors = factors_of(sums, 3)
            before = len(sent)
            for h in common:
                upstream(h, factors)
                back_state(h)
                send_down(h)
            moved = sent[before:]
            del sent[before:]
            for h in (near[0], far):
                arrive(move_up, h)
                attend_prior(h)
            for h in near + (far,):
                upstream(h, factors)
            send(gain_to_first(own))
            back_state(far)
            for move in moved:
                move.wait_send()
            send_down(far)
            for h in range(heads):
                run(local_work(h, factors))
                run(last_work(h))

        if own > 0:
            gain_from_first(own).wait_recv()
            gg_out[...] = gain_back[...]
        for move in sent:
            move.wait_send()

    for own in range(4):
        pl.when(z == own)(functools.partial(program, own))


def write_out(*refs):
    copies = [pltpu.make_async_copy(refs[i], refs[5 + i], refs[10].at[i]) for i in range(5)]
    for copy in copies:
        copy.start()
    for copy in copies:
        copy.wait()


def solution(mesh):
    n_seq, n_tp, n_dp = (mesh.shape[name] for name in ("seq", "tp", "dp"))

    def local(queries, keys, values, out_gain, grad_out):
        shape = queries.shape
        rows, width = shape[0] * shape[1], shape[2]
        heads = width // HD
        chunks = heads * PIECES
        matrix = jax.ShapeDtypeStruct((rows, width), BF16)
        state = pltpu.VMEM((heads, HD, HD), F32)
        page = pltpu.VMEM((rows, width), BF16)
        tile = lambda *lead: pltpu.VMEM((*lead, rows, HD), F32)
        sems = pltpu.SemaphoreType.DMA
        flat = lambda x: x.reshape(rows, width)
        with_help = n_seq == 4 and rows == HD and heads >= 4 and n_tp % 2 == 0
        if with_help:
            body = functools.partial(helped, n_tp, n_dp)
            sums, stats = tile(3), n_seq * n_tp
            early = [tile(9), tile(6), tile(2)]
            early_sems = [sems((9,)), sems((6,))]
            pace = [pltpu.SemaphoreType.REGULAR]
            pages, out_sems, out_space = [], [], pltpu.VMEM
            stat_sems = [sems((3 * n_tp,)), sems((n_seq * n_tp,))]
        else:
            body = functools.partial(kernel, n_seq, n_tp, n_dp)
            sums, stats, early, early_sems, pace = tile(), n_tp, [], [], []
            pages, out_sems, out_space = [page] * 4, [sems((4 * heads + 1,))], pl.ANY
            stat_sems = [sems((max(n_tp - 1, 1),)), sems((max(n_tp - 1, 1),))]
        outs = pl.pallas_call(
            body,
            out_shape=(matrix,) * 4 + (jax.ShapeDtypeStruct((heads, HD), F32),),
            in_specs=[pl.BlockSpec(memory_space=pltpu.HBM)] * 5,
            out_specs=[pl.BlockSpec(memory_space=out_space)] * 5,
            scratch_shapes=[
                page, page, page, pltpu.VMEM((heads, HD), F32), page,
                state, state, state, state,
                pltpu.VMEM((rows, width), F32),
                pltpu.VMEM((heads, rows, rows), BF16), pltpu.VMEM((heads, rows, rows), BF16),
                sums, sums, tile(heads), tile(heads),
                page, *pages,
                *early,
                pltpu.VMEM((stats, 8, rows), F32),
                pltpu.VMEM((n_seq, heads, HD), F32),
                pltpu.VMEM((n_dp, heads, HD), F32),
                pltpu.VMEM((heads, HD), F32), pltpu.VMEM((heads, HD), F32),
                sems((5,)), *out_sems,
                sems((chunks,)), sems((chunks,)), sems((chunks,)), sems((chunks,)),
                *early_sems,
                *stat_sems,
                sems((n_seq,)), sems((n_seq,)),
                sems((max(n_dp - 1, 1),)), sems((max(n_dp - 1, 1),)),
                sems((n_seq,)), sems((n_seq,)), *pace,
            ],
            compiler_params=pltpu.CompilerParams(
                collective_id=0, has_side_effects=True, vmem_limit_bytes=32 << 20
            ),
        )(
            *(
                pltpu.with_memory_space_constraint(x, pltpu.HBM)
                for x in (
                    flat(queries), flat(keys), flat(values),
                    out_gain.reshape(heads, HD), flat(grad_out),
                )
            )
        )
        outs = pl.pallas_call(
            write_out,
            out_shape=tuple(jax.ShapeDtypeStruct(x.shape, x.dtype) for x in outs),
            in_specs=[pl.BlockSpec(memory_space=pl.ANY)] * 5,
            out_specs=[pl.BlockSpec(memory_space=pl.ANY)] * 5,
            scratch_shapes=[sems((5,))],
            compiler_params=pltpu.CompilerParams(vmem_limit_bytes=8 << 20),
        )(*outs)
        return tuple(x.reshape(shape) for x in outs[:4]) + (outs[4].reshape(width),)

    spec = P("dp", "seq", "tp")
    return jax.shard_map(
        local,
        mesh=mesh,
        in_specs=(spec, spec, spec, P("tp"), spec),
        out_specs=(spec, spec, spec, spec, P("tp")),
        check_vma=False,
    )
```

```python
import functools

import jax
import jax.numpy as jnp
from jax import lax
from jax.experimental import pallas as pl
from jax.experimental.pallas import tpu as pltpu
from jax.sharding import PartitionSpec as P

HD = 128
HID = 4096
EPSILON = 1e-06
PIECES = 4
PART = HD // PIECES
MESH = pl.DeviceIdType.MESH
F32 = jnp.float32
BF16 = jnp.bfloat16


def dot(a, b, ca, cb):
    return lax.dot_general(a, b, (((ca,), (cb,)), ((), ())), preferred_element_type=F32)


def split(x):
    high = x.astype(BF16)
    return high, (x - high.astype(F32)).astype(BF16)


def dot_wide(a, x, ca, cb):
    both = jnp.concatenate(split(x), axis=cb)
    return dot(jnp.concatenate((a, a), axis=ca), both, ca, cb)


def kernel(
    n_seq, n_tp, n_dp,
    q_in, k_in, v_in, gain_in, g_in,
    normed_out, dq_out, dk_out, dv_out, gg_out,
    q_ref, k_ref, v_ref, gain_ref, g_ref,
    prior, total, later, total_back,
    att, scores, mixed, squares, crossed, dk_part, dv_part, up, normed, dq, dk, dv,
    stat, gain_seq, gain_dp, gg, gain_back,
    in_sem, out_sem,
    up_send, up_recv, down_send, down_recv,
    stat_send, stat_recv, gs_send, gs_recv, gd_send, gd_recv,
    gb_send, gb_recv,
):
    rows, width = q_ref.shape
    heads = width // HD
    z = lax.axis_index("seq")
    t = lax.axis_index("tp")
    d = lax.axis_index("dp")
    first, last = z == 0, z == n_seq - 1
    above = lax.rem(z + 1, n_seq)
    below = lax.rem(z + n_seq - 1, n_seq)

    def head(h):
        return slice(h * HD, (h + 1) * HD)

    def peers(axis, me, size):
        return [{axis: lax.rem(me + i, size)} for i in range(1, size)]

    greeted = peers("tp", t, n_tp) + peers("dp", d, n_dp)
    if n_seq > 1:
        greeted.append({"seq": below})
    barrier = pltpu.get_barrier_semaphore()
    for peer in greeted:
        pl.semaphore_signal(barrier, inc=1, device_id=peer, device_id_type=MESH)

    loads = [
        pltpu.make_async_copy(src, dst, in_sem.at[i])
        for i, (src, dst) in enumerate(
            [(k_in, k_ref), (v_in, v_ref), (q_in, q_ref), (g_in, g_ref), (gain_in, gain_ref)]
        )
    ]
    for load in loads:
        load.start()
    loads[0].wait()
    loads[1].wait()

    def part(p):
        return slice(p * PART, (p + 1) * PART)

    def move_up(h, p):
        i = h * PIECES + p
        return pltpu.make_async_remote_copy(
            src_ref=total.at[h, part(p)], dst_ref=prior.at[h, part(p)],
            send_sem=up_send.at[i], recv_sem=up_recv.at[i],
            device_id={"seq": above}, device_id_type=MESH,
        )

    def move_down(h, p):
        i = h * PIECES + p
        return pltpu.make_async_remote_copy(
            src_ref=total_back.at[h, part(p)], dst_ref=later.at[h, part(p)],
            send_sem=down_send.at[i], recv_sem=down_recv.at[i],
            device_id={"seq": below}, device_id_type=MESH,
        )

    def relay(h, p, mine, come, move, is_first, is_last):
        @pl.when(jnp.logical_and(jnp.logical_not(is_first), jnp.logical_not(is_last)))
        def _():
            move(h, p).wait_recv()
            mine[h, part(p)] = mine[h, part(p)] + come[h, part(p)]
            move(h, p).start()

        @pl.when(jnp.logical_and(is_last, jnp.logical_not(is_first)))
        def _():
            move(h, p).wait_recv()

    def relay_all(mine, come, move, is_first, is_last, slots):
        for h in range(heads):
            for p in range(PIECES):
                relay(h, p, mine, come, move, is_first, is_last)
                for step in slots[h * PIECES + p]:
                    step()

    for h in range(heads):
        total[h] = dot(k_ref[:, head(h)], v_ref[:, head(h)], 0, 0)
        if h == 0:
            pl.semaphore_wait(barrier, len(greeted))
        if n_seq > 1:
            @pl.when(first)
            def _():
                for p in range(PIECES):
                    move_up(h, p).start()

    @pl.when(first)
    def _():
        prior[...] = jnp.zeros_like(prior)

    @pl.when(last)
    def _():
        later[...] = jnp.zeros_like(later)

    loads[2].wait()
    loads[3].wait()
    loads[4].wait()
    causal = lax.broadcasted_iota(jnp.int32, (rows, rows), 0) >= lax.broadcasted_iota(
        jnp.int32, (rows, rows), 1
    )
    def score_of(h):
        score = jnp.where(causal, dot(q_ref[:, head(h)], k_ref[:, head(h)], 1, 1), 0.0)
        scores[h] = score.astype(BF16)

    def attend_block(h):
        att[:, head(h)] = dot(scores[h], v_ref[:, head(h)], 1, 0)

    def attend_prior(h):
        att[:, head(h)] = att[:, head(h)] + dot_wide(q_ref[:, head(h)], prior[h], 1, 0)

    def add_stats(h):
        out = att[:, head(h)]
        square = out * out
        cross = g_ref[:, head(h)].astype(F32) * gain_ref[h:h + 1, :] * out
        squares[...] = square if h == 0 else squares[...] + square
        crossed[...] = cross if h == 0 else crossed[...] + cross

    slots = [[] for _ in range(heads * PIECES)]
    for h in range(heads):
        slots[h * PIECES].append(functools.partial(score_of, h))
        slots[h * PIECES + 1].append(functools.partial(attend_block, h))
        if h > 0:
            slots[h * PIECES + 2].append(functools.partial(attend_prior, h - 1))
            slots[h * PIECES + 3].append(functools.partial(add_stats, h - 1))
    relay_all(total, prior, move_up, first, last, slots)
    attend_prior(heads - 1)
    add_stats(heads - 1)

    stat[t, 0:1, :] = jnp.sum(squares[...].T, axis=0, keepdims=True)
    stat[t, 1:2, :] = jnp.sum(crossed[...].T, axis=0, keepdims=True)

    def all_send(buffer, axis, me, size, send, recv):
        return [
            pltpu.make_async_remote_copy(
                src_ref=buffer.at[me], dst_ref=buffer.at[me],
                send_sem=send.at[i - 1], recv_sem=recv.at[i - 1],
                device_id={axis: lax.rem(me + i, size)}, device_id_type=MESH,
            )
            for i in range(1, size)
        ]

    stat_moves = all_send(stat, "tp", t, n_tp, stat_send, stat_recv)
    for move in stat_moves:
        move.start()
    for move in stat_moves:
        move.wait_recv()
    sums = stat[0, 0:2, :]
    for i in range(1, n_tp):
        sums = sums + stat[i, 0:2, :]
    scale_row = lax.rsqrt(sums[0:1] / HID + EPSILON)
    factor_row = scale_row * scale_row * scale_row * sums[1:2] / HID
    scale = jnp.broadcast_to(scale_row, (HD, rows)).T
    factor = jnp.broadcast_to(factor_row, (HD, rows)).T

    def upstream(h):
        out = att[:, head(h)]
        grad = g_ref[:, head(h)].astype(F32)
        scaled = grad * scale
        up[:, head(h)] = (gain_ref[h:h + 1, :] * scaled - out * factor).astype(BF16)
        gain_seq[z, h:h + 1, :] = jnp.sum(scaled * out, axis=0, keepdims=True)

    def back_state(h):
        total_back[h] = dot(q_ref[:, head(h)], up[:, head(h)], 0, 0)
        if n_seq > 1:
            @pl.when(last)
            def _():
                for p in range(PIECES):
                    move_down(h, p).start()

    upstream(0)
    back_state(0)
    for h in range(1, heads):
        upstream(h)

    def gain_to_first(source):
        return pltpu.make_async_remote_copy(
            src_ref=gain_seq.at[source], dst_ref=gain_seq.at[source],
            send_sem=gs_send.at[source], recv_sem=gs_recv.at[source],
            device_id={"seq": 0}, device_id_type=MESH,
        )

    def gain_from_first(target):
        return pltpu.make_async_remote_copy(
            src_ref=gg, dst_ref=gain_back,
            send_sem=gb_send.at[target], recv_sem=gb_recv.at[target],
            device_id={"seq": target}, device_id_type=MESH,
        )

    @pl.when(jnp.logical_not(first))
    def _():
        gain_to_first(z).start()

    for h in range(1, heads):
        back_state(h)

    dp_moves = all_send(gain_dp, "dp", d, n_dp, gd_send, gd_recv)
    stores = []

    def store(src, dst):
        copy = pltpu.make_async_copy(src, dst, out_sem.at[len(stores)])
        copy.start()
        stores.append(copy)

    def normed_of(h):
        normed[:, head(h)] = (att[:, head(h)] * scale * gain_ref[h:h + 1, :]).astype(BF16)
        store(normed.at[:, head(h)], normed_out.at[:, head(h)])

    def mixed_of(h):
        mix = jnp.where(causal, dot(up[:, head(h)], v_ref[:, head(h)], 1, 1), 0.0)
        mixed[h] = mix.astype(BF16)

    def dq_of(h):
        dq[:, head(h)] = (
            dot(mixed[h], k_ref[:, head(h)], 1, 0) + dot_wide(up[:, head(h)], prior[h], 1, 1)
        ).astype(BF16)
        store(dq.at[:, head(h)], dq_out.at[:, head(h)])

    def block_parts(h):
        dk_part[h] = dot(mixed[h], q_ref[:, head(h)], 0, 0)
        dv_part[h] = dot(scores[h], up[:, head(h)], 0, 0)

    def dk_of(h):
        wide = dot_wide(v_ref[:, head(h)], later[h], 1, 1)
        dk[:, head(h)] = (dk_part[h] + wide).astype(BF16)
        store(dk.at[:, head(h)], dk_out.at[:, head(h)])

    def dv_of(h):
        wide = dot_wide(k_ref[:, head(h)], later[h], 1, 0)
        dv[:, head(h)] = (dv_part[h] + wide).astype(BF16)
        store(dv.at[:, head(h)], dv_out.at[:, head(h)])

    def gain_middle():
        @pl.when(first)
        def _():
            for source in range(1, n_seq):
                gain_to_first(source).wait_recv()
            gain_sum = gain_seq[0]
            for i in range(1, n_seq):
                gain_sum = gain_sum + gain_seq[i]
            gain_dp[d] = gain_sum
            for move in dp_moves:
                move.start()

    def gain_end():
        @pl.when(first)
        def _():
            for move in dp_moves:
                move.wait_recv()
            gain_sum = gain_dp[0]
            for i in range(1, n_dp):
                gain_sum = gain_sum + gain_dp[i]
            gg[...] = gain_sum
            for target in range(1, n_seq):
                gain_from_first(target).start()

    block_work = [
        functools.partial(work, h)
        for h in range(heads)
        for work in (mixed_of, dq_of, block_parts, normed_of)
    ]
    half = 2 * heads
    for step in block_work[:half]:
        step()
    slots = [[] for _ in range(heads * PIECES)]
    for h in range(heads):
        if h > 0:
            slots[h * PIECES].append(functools.partial(dk_of, h - 1))
            slots[h * PIECES + 1].append(functools.partial(dv_of, h - 1))
        slots[h * PIECES + 2].append(block_work[half + 2 * h])
        slots[h * PIECES + 3].append(block_work[half + 2 * h + 1])
    slots[0].append(gain_middle)
    slots[heads // 4 * PIECES].append(gain_end)
    relay_all(total_back, later, move_down, last, first, slots)
    dk_of(heads - 1)
    dv_of(heads - 1)

    gg_copy = pltpu.make_async_copy(gg, gg_out, out_sem.at[4 * heads])

    @pl.when(first)
    def _():
        gg_copy.start()
        for move in dp_moves:
            move.wait_send()
        for target in range(1, n_seq):
            gain_from_first(target).wait_send()

    back_copy = pltpu.make_async_copy(gain_back, gg_out, out_sem.at[4 * heads])

    @pl.when(jnp.logical_not(first))
    def _():
        gain_from_first(z).wait_recv()
        back_copy.start()
        gain_to_first(z).wait_send()

    for move in stat_moves:
        move.wait_send()
    if n_seq > 1:
        @pl.when(jnp.logical_not(last))
        def _():
            for h in range(heads):
                for p in range(PIECES):
                    move_up(h, p).wait_send()

        @pl.when(jnp.logical_not(first))
        def _():
            for h in range(heads):
                for p in range(PIECES):
                    move_down(h, p).wait_send()
    for copy in stores:
        copy.wait()

    @pl.when(first)
    def _():
        gg_copy.wait()

    @pl.when(jnp.logical_not(first))
    def _():
        back_copy.wait()


def helped(
    n_tp, n_dp,
    q_in, k_in, v_in, gain_in, g_in,
    normed_out, dq_out, dk_out, dv_out, gg_out,
    q_ref, k_ref, v_ref, gain_ref, g_ref,
    prior, total, later, total_back,
    att, scores, mixed, squares, crossed, dk_part, dv_part, up,
    early_out, early_in, help_att,
    stat, gain_seq, gain_dp, gg, gain_back,
    in_sem,
    up_send, up_recv, down_send, down_recv,
    early_send, early_recv,
    stat_send, stat_recv, gs_send, gs_recv, gd_send, gd_recv,
    gb_send, gb_recv, pace,
):
    rows, width = q_ref.shape
    heads = width // HD
    far, near = heads - 1, (heads - 2, heads - 3)
    common = tuple(range(heads - 3))
    order_down = (far,) + near + common
    z = lax.axis_index("seq")
    t = lax.axis_index("tp")
    d = lax.axis_index("dp")
    slot = z * n_tp + t

    def head(h):
        return slice(h * HD, (h + 1) * HD)

    def part(p):
        return slice(p * PART, (p + 1) * PART)

    def tp_peer(i):
        return lax.rem(t + i, n_tp)

    causal = lax.broadcasted_iota(jnp.int32, (rows, rows), 0) >= lax.broadcasted_iota(
        jnp.int32, (rows, rows), 1
    )
    loads = [
        pltpu.make_async_copy(src, dst, in_sem.at[i])
        for i, (src, dst) in enumerate(
            [(k_in, k_ref), (v_in, v_ref), (q_in, q_ref), (g_in, g_ref), (gain_in, gain_ref)]
        )
    ]

    def program(own):
        barrier = pltpu.get_barrier_semaphore()
        greeted = [{"tp": tp_peer(i)} for i in range(1, n_tp)]
        heard = len(greeted)
        if own == 0:
            greeted += [{"dp": lax.rem(d + i, n_dp)} for i in range(1, n_dp)]
            heard = len(greeted) + 1
        else:
            heard += 2
        greeted += [{"seq": i} for i in ((1,), (0, 2, 3), (1, 3), (2,))[own]]
        for peer in greeted:
            pl.semaphore_signal(barrier, inc=1, device_id=peer, device_id_type=MESH)
        for load in loads:
            load.start()

        sent = []

        def send(move):
            move.start()
            sent.append(move)

        def move_up(h, p):
            i = h * PIECES + p
            return pltpu.make_async_remote_copy(
                src_ref=total.at[h, part(p)], dst_ref=prior.at[h, part(p)],
                send_sem=up_send.at[i], recv_sem=up_recv.at[i],
                device_id={"seq": min(own + 1, 3)}, device_id_type=MESH,
            )

        def move_down(h, p):
            i = h * PIECES + p
            return pltpu.make_async_remote_copy(
                src_ref=total_back.at[h, part(p)], dst_ref=later.at[h, part(p)],
                send_sem=down_send.at[i], recv_sem=down_recv.at[i],
                device_id={"seq": max(own - 1, 0)}, device_id_type=MESH,
            )

        def arrive(move, h):
            for p in range(PIECES):
                move(h, p).wait_recv()

        def move_early(i, j, target):
            return pltpu.make_async_remote_copy(
                src_ref=early_out.at[i], dst_ref=early_in.at[j],
                send_sem=early_send.at[i], recv_sem=early_recv.at[j],
                device_id={"seq": target}, device_id_type=MESH,
            )

        def early_arrive(j, source):
            move_early(0, j, source).wait_recv()

        def total_of(h):
            total[h] = dot(k_ref[:, head(h)], v_ref[:, head(h)], 0, 0)

        def score_of(h):
            score = jnp.where(causal, dot(q_ref[:, head(h)], k_ref[:, head(h)], 1, 1), 0.0)
            scores[h] = score.astype(BF16)

        def attend_block(h):
            att[:, head(h)] = dot(scores[h], v_ref[:, head(h)], 1, 0)

        def attend_prior(h):
            att[:, head(h)] = att[:, head(h)] + dot_wide(q_ref[:, head(h)], prior[h], 1, 0)

        counted = set()

        def count(i, out, weighted):
            square, cross = out * out, weighted * out
            squares[i] = squares[i] + square if i in counted else square
            crossed[i] = crossed[i] + cross if i in counted else cross
            counted.add(i)

        def add_stats(h):
            count(0, att[:, head(h)], g_ref[:, head(h)].astype(F32) * gain_ref[h:h + 1, :])

        def send_early(h, first, slots, target, state=None):
            early_out[first] = q_ref[:, head(h)].astype(F32)
            send(move_early(first, slots, target))
            early_out[first + 1] = g_ref[:, head(h)].astype(F32)
            send(move_early(first + 1, slots + 1, target))
            score_of(h)
            local = dot(scores[h], v_ref[:, head(h)], 1, 0)
            att[:, head(h)] = local
            if state is not None:
                early_arrive(state, 2)
                local = local + dot_wide(q_ref[:, head(h)], early_in[state], 1, 0)
            early_out[first + 2] = local
            send(move_early(first + 2, slots + 2, target))

        def help_attend(j, first, h, state, i):
            early_arrive(first, own + i)
            wide = dot_wide(early_in[first].astype(BF16), state, 1, 0)
            for n in (first + 1, first + 2):
                early_arrive(n, own + i)
            out = early_in[first + 2] + wide
            help_att[j] = out
            count(i, out, early_in[first + 1] * gain_ref[h:h + 1, :])

        def help_back(j, first, h, factors):
            scaled = early_in[first + 1] * factors[0]
            grad = (gain_ref[h:h + 1, :] * scaled - help_att[j] * factors[1]).astype(BF16)
            return dot(early_in[first].astype(BF16), grad, 0, 0)

        def relay(mine, come, move, order, slots, start=True):
            slots = list(slots)
            for h in order:
                for p in range(PIECES):
                    move(h, p).wait_recv()
                    mine[h, part(p)] = mine[h, part(p)] + come[h, part(p)]
                    send(move(h, p))
                    if slots:
                        slots.pop(0)()
            for step in slots:
                step()

        def put_stats(blocks):
            for i in blocks:
                b = 2 * (own + i)
                stat[slot, b:b + 1, :] = jnp.sum(squares[i].T, axis=0, keepdims=True)
                stat[slot, b + 1:b + 2, :] = jnp.sum(crossed[i].T, axis=0, keepdims=True)

        def stat_move(n, target, i):
            return pltpu.make_async_remote_copy(
                src_ref=stat.at[slot], dst_ref=stat.at[slot],
                send_sem=stat_send.at[n], recv_sem=stat_recv.at[slot],
                device_id={"seq": target, "tp": tp_peer(i)}, device_id_type=MESH,
            )

        def send_stats():
            n = 0
            for target in ((0,), (1, 3, 2), (2, 3, 1), (3, 2, 1))[own]:
                for i in range(1 if target == own else 0, n_tp):
                    send(stat_move(n, target, i))
                    n += 1

        def sum_stats(source):
            for i in range(1 if source == own else 0, n_tp):
                s = source * n_tp + tp_peer(i)
                pltpu.make_async_remote_copy(
                    src_ref=stat.at[s], dst_ref=stat.at[s],
                    send_sem=stat_send.at[0], recv_sem=stat_recv.at[s],
                    device_id={"tp": tp_peer(1)}, device_id_type=MESH,
                ).wait_recv()
            total_stat = stat[source * n_tp]
            for i in range(1, n_tp):
                total_stat = total_stat + stat[source * n_tp + i]
            return total_stat

        def factors_of(sums, b):
            scale = lax.rsqrt(sums[2 * b:2 * b + 1] / HID + EPSILON)
            factor = scale * scale * scale * sums[2 * b + 1:2 * b + 2] / HID
            return tuple(jnp.broadcast_to(x, (HD, rows)).T for x in (scale, factor))

        def upstream(h, factors):
            out = att[:, head(h)]
            scaled = g_ref[:, head(h)].astype(F32) * factors[0]
            up[:, head(h)] = (gain_ref[h:h + 1, :] * scaled - out * factors[1]).astype(BF16)
            gain_seq[own, h:h + 1, :] = jnp.sum(scaled * out, axis=0, keepdims=True)

        def back_state(h):
            total_back[h] = dot(q_ref[:, head(h)], up[:, head(h)], 0, 0)

        def send_down(h):
            for p in range(PIECES):
                send(move_down(h, p))

        def gain_to_first(source):
            return pltpu.make_async_remote_copy(
                src_ref=gain_seq.at[source], dst_ref=gain_seq.at[source],
                send_sem=gs_send.at[source], recv_sem=gs_recv.at[source],
                device_id={"seq": 0}, device_id_type=MESH,
            )

        def gain_from_first(target):
            return pltpu.make_async_remote_copy(
                src_ref=gg, dst_ref=gain_back,
                send_sem=gb_send.at[target], recv_sem=gb_recv.at[target],
                device_id={"seq": target}, device_id_type=MESH,
            )

        def normed_of(h, factors):
            normed_out[:, head(h)] = (
                att[:, head(h)] * factors[0] * gain_ref[h:h + 1, :]
            ).astype(BF16)

        def mixed_of(h):
            mix = jnp.where(causal, dot(up[:, head(h)], v_ref[:, head(h)], 1, 1), 0.0)
            mixed[h] = mix.astype(BF16)

        def dq_of(h):
            wide = dot(mixed[h], k_ref[:, head(h)], 1, 0)
            if own > 0:
                wide = wide + dot_wide(up[:, head(h)], prior[h], 1, 1)
            dq_out[:, head(h)] = wide.astype(BF16)

        def block_parts(h):
            dk_part[h] = dot(mixed[h], q_ref[:, head(h)], 0, 0)
            dv_part[h] = dot(scores[h], up[:, head(h)], 0, 0)

        def dk_of(h):
            wide = dk_part[h]
            if own < 3:
                wide = wide + dot_wide(v_ref[:, head(h)], later[h], 1, 1)
            dk_out[:, head(h)] = wide.astype(BF16)

        def dv_of(h):
            wide = dv_part[h]
            if own < 3:
                wide = wide + dot_wide(k_ref[:, head(h)], later[h], 1, 0)
            dv_out[:, head(h)] = wide.astype(BF16)

        def local_work(h, factors):
            return [
                functools.partial(mixed_of, h),
                functools.partial(dq_of, h),
                functools.partial(block_parts, h),
                functools.partial(normed_of, h, factors),
            ]

        def last_work(h):
            return [functools.partial(dk_of, h), functools.partial(dv_of, h)]

        def run(steps):
            for step in steps:
                step()

        def local_attention(order):
            for h in order:
                score_of(h)
                attend_block(h)

        def own_part(h):
            return [functools.partial(attend_prior, h), functools.partial(add_stats, h)]

        def forward_slots(order):
            slots = [lambda: None] * PIECES
            for h in order:
                slots += own_part(h) + [lambda: None] * (PIECES - 2)
            return slots

        stat[slot] = jnp.zeros_like(stat[slot])
        for load in loads:
            load.wait()

        if own == 0:
            for h in range(heads):
                total_of(h)
                if h == 0:
                    pl.semaphore_wait(barrier, heard)
                if h in common:
                    for p in range(PIECES):
                        send(move_up(h, p))
            first_moves = list(sent)
            sent.clear()
            sent += [move_up(h, p) for h in range(heads - 3, heads) for p in range(PIECES)]
            odd = t % 2 == 1

            @pl.when(odd)
            def _():
                pl.semaphore_wait(pace, 1)
                for move in sent:
                    move.start()
                for move in first_moves:
                    move.wait_send()

            @pl.when(jnp.logical_not(odd))
            def _():
                for move in sent:
                    move.start()
                for move in first_moves[:-12]:
                    move.wait_send()
                pl.semaphore_signal(
                    pace, inc=1, device_id={"tp": t + 1}, device_id_type=MESH
                )
                for move in first_moves[-12:]:
                    move.wait_send()

            local_attention(range(heads))
            for h in range(heads):
                add_stats(h)
            put_stats((0,))
            send_stats()
            factors = factors_of(sum_stats(0), 0)
            for h in range(heads):
                upstream(h, factors)
            for h in range(heads):
                run(local_work(h, factors))
            gains = [{"dp": lax.rem(d + i, n_dp)} for i in range(1, n_dp)]
            gain_moves = [
                pltpu.make_async_remote_copy(
                    src_ref=gain_dp.at[d], dst_ref=gain_dp.at[d],
                    send_sem=gd_send.at[i], recv_sem=gd_recv.at[i],
                    device_id=peer, device_id_type=MESH,
                )
                for i, peer in enumerate(gains)
            ]
            for n, h in enumerate(order_down):
                arrive(move_down, h)
                run(last_work(h))
                if n == 0:
                    for source in range(1, 4):
                        gain_to_first(source).wait_recv()
                    gain_dp[d] = (gain_seq[0] + gain_seq[1]) + (gain_seq[2] + gain_seq[3])
                    for move in gain_moves:
                        send(move)
                if n == 2:
                    for move in gain_moves:
                        move.wait_recv()
                    gain_sum = gain_dp[0]
                    for i in range(1, n_dp):
                        gain_sum = gain_sum + gain_dp[i]
                    gg[...] = gain_sum
                    for target in range(1, 4):
                        send(gain_from_first(target))
                    gg_out[...] = gain_sum

        if own == 1:
            pl.semaphore_wait(barrier, heard)
            for h in range(heads):
                total_of(h)
            local_attention(range(heads))
            relay(total, prior, move_up, range(heads), forward_slots(range(heads)))
            help_attend(0, 3, far, total[far], 1)
            help_attend(1, 0, far, total[far], 2)
            put_stats((0, 1, 2))
            send_stats()
            sums = sum_stats(1)
            factors = factors_of(sums, 1)
            for h in order_down:
                upstream(h, factors)
                back_state(h)
            send(gain_to_first(own))
            run(local_work(far, factors))
            sums = sums + sum_stats(2)
            beyond = help_back(0, 3, far, factors_of(sums, 2))
            total_back[far] = total_back[far] + beyond
            sums = sums + sum_stats(3)
            last = help_back(1, 0, far, factors_of(sums, 3))
            total_back[far] = total_back[far] + last
            send_down(far)
            later[far] = beyond + last
            run(last_work(far))
            steps = []
            for h in near + common:
                steps += local_work(h, factors)
            run(steps[:2])
            relay(total_back, later, move_down, near + common, steps[2:])
            for h in near + common:
                run(last_work(h))

        if own == 2:
            total_of(far)
            early_out[3] = total[far]
            pl.semaphore_wait(barrier, heard)
            send(move_early(3, 0, 3))
            send_early(far, 0, 3, 1)
            for h in range(heads - 1):
                total_of(h)
            local_attention(range(heads - 1))
            relay(total, prior, move_up, range(heads - 1), forward_slots(range(heads - 2)))
            run(own_part(near[0]))
            help_attend(0, 0, near[0], total[near[0]], 1)
            put_stats((0,))
            help_attend(1, 3, near[1], total[near[1]], 1)
            put_stats((1,))
            send_stats()
            relay(total, prior, move_up, (far,), ())
            attend_prior(far)
            sums = sum_stats(1) + sum_stats(2)
            factors = factors_of(sums, 2)
            for h in near:
                upstream(h, factors)
                back_state(h)
            sums = sums + sum_stats(3)
            ahead = factors_of(sums, 3)
            for j, h in enumerate(near):
                beyond = help_back(j, 3 * j, h, ahead)
                total_back[h] = total_back[h] + beyond
                send_down(h)
                later[h] = beyond
            for h in common:
                upstream(h, factors)
                back_state(h)
            upstream(far, factors)
            send(gain_to_first(own))
            steps = []
            for h in near:
                steps += local_work(h, factors) + last_work(h)
            for h in common + (far,):
                steps += local_work(h, factors)
            relay(total_back, later, move_down, common, steps)
            for h in common:
                run(last_work(h))
            arrive(move_down, far)
            run(last_work(far))

        if own == 3:
            pl.semaphore_wait(barrier, heard)
            send_early(near[0], 3, 0, 2)
            send_early(far, 0, 0, 1, 0)
            send_early(near[1], 6, 3, 2)
            local_attention(common)
            for h in common:
                arrive(move_up, h)
                attend_prior(h)
                add_stats(h)
            put_stats((0,))
            send_stats()
            arrive(move_up, near[1])
            attend_prior(near[1])
            sums = sum_stats(1) + sum_stats(2)
            sums = sums + sum_stats(3)
            factors = factors_of(sums, 3)
            before = len(sent)
            for h in common:
                upstream(h, factors)
                back_state(h)
                send_down(h)
            moved = sent[before:]
            del sent[before:]
            for h in (near[0], far):
                arrive(move_up, h)
                attend_prior(h)
            for h in near + (far,):
                upstream(h, factors)
            send(gain_to_first(own))
            back_state(far)
            for move in moved:
                move.wait_send()
            send_down(far)
            for h in range(heads):
                run(local_work(h, factors))
                run(last_work(h))

        if own > 0:
            gain_from_first(own).wait_recv()
            gg_out[...] = gain_back[...]
        for move in sent:
            move.wait_send()

    for own in range(4):
        pl.when(z == own)(functools.partial(program, own))


def write_out(*refs):
    copies = [pltpu.make_async_copy(refs[i], refs[5 + i], refs[10].at[i]) for i in range(5)]
    for copy in copies:
        copy.start()
    for copy in copies:
        copy.wait()


def solution(mesh):
    n_seq, n_tp, n_dp = (mesh.shape[name] for name in ("seq", "tp", "dp"))

    def local(queries, keys, values, out_gain, grad_out):
        shape = queries.shape
        rows, width = shape[0] * shape[1], shape[2]
        heads = width // HD
        chunks = heads * PIECES
        matrix = jax.ShapeDtypeStruct((rows, width), BF16)
        state = pltpu.VMEM((heads, HD, HD), F32)
        page = pltpu.VMEM((rows, width), BF16)
        tile = lambda *lead: pltpu.VMEM((*lead, rows, HD), F32)
        sems = pltpu.SemaphoreType.DMA
        flat = lambda x: x.reshape(rows, width)
        with_help = n_seq == 4 and rows == HD and heads >= 4 and n_tp % 2 == 0
        if with_help:
            body = functools.partial(helped, n_tp, n_dp)
            sums, stats = tile(3), n_seq * n_tp
            early = [tile(9), tile(6), tile(2)]
            early_sems = [sems((9,)), sems((6,))]
            pace = [pltpu.SemaphoreType.REGULAR]
            pages, out_sems, out_space = [], [], pltpu.VMEM
            stat_sems = [sems((3 * n_tp,)), sems((n_seq * n_tp,))]
        else:
            body = functools.partial(kernel, n_seq, n_tp, n_dp)
            sums, stats, early, early_sems, pace = tile(), n_tp, [], [], []
            pages, out_sems, out_space = [page] * 4, [sems((4 * heads + 1,))], pl.ANY
            stat_sems = [sems((max(n_tp - 1, 1),)), sems((max(n_tp - 1, 1),))]
        outs = pl.pallas_call(
            body,
            out_shape=(matrix,) * 4 + (jax.ShapeDtypeStruct((heads, HD), F32),),
            in_specs=[pl.BlockSpec(memory_space=pltpu.HBM)] * 5,
            out_specs=[pl.BlockSpec(memory_space=out_space)] * 5,
            scratch_shapes=[
                page, page, page, pltpu.VMEM((heads, HD), F32), page,
                state, state, state, state,
                pltpu.VMEM((rows, width), F32),
                pltpu.VMEM((heads, rows, rows), BF16), pltpu.VMEM((heads, rows, rows), BF16),
                sums, sums, tile(heads), tile(heads),
                page, *pages,
                *early,
                pltpu.VMEM((stats, 8, rows), F32),
                pltpu.VMEM((n_seq, heads, HD), F32),
                pltpu.VMEM((n_dp, heads, HD), F32),
                pltpu.VMEM((heads, HD), F32), pltpu.VMEM((heads, HD), F32),
                sems((5,)), *out_sems,
                sems((chunks,)), sems((chunks,)), sems((chunks,)), sems((chunks,)),
                *early_sems,
                *stat_sems,
                sems((n_seq,)), sems((n_seq,)),
                sems((max(n_dp - 1, 1),)), sems((max(n_dp - 1, 1),)),
                sems((n_seq,)), sems((n_seq,)), *pace,
            ],
            compiler_params=pltpu.CompilerParams(
                collective_id=0, has_side_effects=True, vmem_limit_bytes=32 << 20
            ),
        )(
            *(
                pltpu.with_memory_space_constraint(x, pltpu.HBM)
                for x in (
                    flat(queries), flat(keys), flat(values),
                    out_gain.reshape(heads, HD), flat(grad_out),
                )
            )
        )
        outs = pl.pallas_call(
            write_out,
            out_shape=tuple(jax.ShapeDtypeStruct(x.shape, x.dtype) for x in outs),
            in_specs=[pl.BlockSpec(memory_space=pl.ANY)] * 5,
            out_specs=[pl.BlockSpec(memory_space=pl.ANY)] * 5,
            scratch_shapes=[sems((5,))],
            compiler_params=pltpu.CompilerParams(vmem_limit_bytes=8 << 20),
        )(*outs)
        return tuple(x.reshape(shape) for x in outs[:4]) + (outs[4].reshape(width),)

    spec = P("dp", "seq", "tp")
    return jax.shard_map(
        local,
        mesh=mesh,
        in_specs=(spec, spec, spec, P("tp"), spec),
        out_specs=(spec, spec, spec, spec, P("tp")),
        check_vma=False,
    )
```
